128 devices in a mesh: grp: 4 (over y), in: 32 (over z, x, core).
Axes of the slice: x: 4, y: 4, z: 4, core: 2. Of those that a mesh axis runs over, the one named last changes fastest.
Arguments:
- unfolding: float32 [1024, 524288], P(None, ('grp', 'in')), may hold values from -300 to 300
- start_basis: float32 [1024, 128], replicated, may hold values from -6 to 6
Outputs:
- factor: float32 [1024, 128], replicated
- core_block: float32 [128, 524288], P(None, ('grp', 'in'))
The draws below stay inside these ranges and needn't reach their ends.
All inputs are finite; a program needn't handle non-finite values.
Results may differ from the reference program's by a relative error of at most 0.0003.
Values sent between devices are 32-bit elements; how exact they have to be, the bound alone decides.
A program may use at most 128 MiB of HBM per device.

```python
import jax
import jax.numpy as jnp
from jax import lax

I1 = 1024
RANK = 128
ITERS = 3
COLS = 524288


def draw_unfolding(key, part):
    key_rows, key_cols, key_left, key_right, key_noise = jax.random.split(key, 5)
    row_scale = jnp.exp(jax.random.uniform(key_rows, (I1, 1), jnp.float32, 0.0, jnp.log(10.0)))
    ramp = 1.0 + 2.0 * jnp.arange(COLS, dtype=jnp.float32) / COLS
    col_scale = jnp.exp(jax.random.uniform(key_cols, (1, COLS), jnp.float32, 0.0, jnp.log(2.0))) * ramp[None, :]
    decay = jnp.exp(-2.0 * jnp.arange(RANK, dtype=jnp.float32) / RANK)
    left = jnp.clip(jax.random.normal(key_left, (I1, RANK), jnp.float32), -5.0, 5.0)
    right = jnp.clip(jax.random.normal(key_right, (COLS, RANK), jnp.float32), -5.0, 5.0)
    noise = 0.1 * jnp.clip(jax.random.normal(key_noise, (I1, COLS), jnp.float32), -5.0, 5.0)
    signal = jnp.dot(left * decay[None, :], right.T, precision=lax.Precision.HIGHEST, preferred_element_type=jnp.float32) / jnp.sqrt(jnp.float32(RANK))
    return jnp.clip(row_scale * col_scale * (signal + noise), -300.0, 300.0).astype(jnp.float32)


def centred(rng, extent, width, reach, held_as=jnp.bfloat16):
    result = jax.random.normal(rng, extent, jnp.float32) * width
    return jnp.minimum(jnp.maximum(result, -reach), reach).astype(held_as)


def setup_inputs(seed: int = 0) -> dict:
    splits = jax.random.split(jax.random.key(seed), 3)
    unfolding = draw_unfolding(jax.random.fold_in(splits[2], 71), 0)
    start_basis = centred(splits[1], (I1, RANK), 1.0, 6.0, jnp.float32)
    return {"unfolding": unfolding, "start_basis": start_basis}


def orthonormal(image):
    inner = jnp.dot(image.T.astype(jnp.float32), image.astype(jnp.float32), precision=lax.Precision.HIGHEST, preferred_element_type=jnp.float32)
    lower = jnp.linalg.cholesky(inner)
    return lax.linalg.triangular_solve(lower, image, left_side=False, lower=True, transpose_a=True)

def reference(unfolding, start_basis):
    gram = lax.dot_general(unfolding.astype(jnp.float32), unfolding.astype(jnp.float32), (((1,), (1,)), ((), ())), precision=lax.Precision.HIGHEST, preferred_element_type=jnp.float32)
    basis = start_basis
    for step in range(ITERS):
        image = jnp.dot(gram.astype(jnp.float32), basis.astype(jnp.float32), precision=lax.Precision.HIGHEST, preferred_element_type=jnp.float32)
        basis = orthonormal(image)
    core_block = jnp.dot(basis.T.astype(jnp.float32), unfolding.astype(jnp.float32), precision=lax.Precision.HIGHEST, preferred_element_type=jnp.float32)
    return (basis, core_block)
```

```python
import functools

import jax
import jax.numpy as jnp
from jax import lax
from jax.experimental import pallas as pl
from jax.experimental.pallas import tpu as pltpu
from jax.sharding import PartitionSpec as P

HI = lax.Precision.HIGHEST
F32 = jnp.float32
BF = jnp.bfloat16

def split(x):
    hi = x.astype(BF)
    return hi, (x - hi.astype(F32)).astype(BF)

def dg(a, b, ca, cb):
    return lax.dot_general(a, b, (((ca,), (cb,)), ((), ())), preferred_element_type=F32)

def eliminate(a_ref, q_ref, w_ref):
    sub = lax.broadcasted_iota(jnp.int32, (8, 128), 0)
    lane = lax.broadcasted_iota(jnp.int32, (8, 128), 1)
    M = [a_ref[8*p:8*p+8, :] for p in range(16)]
    Q = [jnp.where(lane == sub + 8*p, 1.0, 0.0).astype(F32) for p in range(16)]
    for p in range(16):
        P, R = M[p], Q[p]
        cols = [jnp.broadcast_to(P[:, 8*p+c:8*p+c+1], (8, 128)) for c in range(8)]
        piv = []
        recs = []
        for r in range(8):
            d = jnp.broadcast_to(cols[r][r:r+1, :], (8, 128))
            rec = 1.0 / d
            piv.append(d); recs.append(rec)
            if r == 7: break
            m = jnp.where(sub > r, cols[r] * rec, 0.0)
            for c in range(r+1, 8):
                cols[c] = cols[c] - m * jnp.broadcast_to(cols[c][r:r+1, :], (8, 128))
            P = P - m * jnp.broadcast_to(P[r:r+1, :], (8, 128))
            R = R - m * jnp.broadcast_to(R[r:r+1, :], (8, 128))
        dv = piv[7]; rv = recs[7]
        for r in range(7):
            dv = jnp.where(sub == r, piv[r], dv)
            rv = jnp.where(sub == r, recs[r], rv)
        w_ref[8*p:8*p+8, :] = R * (1.0 / jnp.sqrt(dv))
        if p < 15:
            T = jnp.transpose(P * rv)
            pr = [jnp.broadcast_to(P[r:r+1, :], (8, 128)) for r in range(8)]
            qr = [jnp.broadcast_to(R[r:r+1, :], (8, 128)) for r in range(8)]
            for i in range(p+1, 16):
                for r in range(8):
                    mm = jnp.broadcast_to(T[8*i:8*i+8, r:r+1], (8, 128))
                    M[i] = M[i] - mm * pr[r]
                    Q[i] = Q[i] - mm * qr[r]

def k2_kernel(x_ref, s_ref, f_ref, ghi, glo, img, a_ref, q_ref, w_ref, *, iters=3):
    k = 0
    for i in range(4):
        for j in range(i, 4):
            blk = jnp.concatenate([x_ref[k, :256, :], x_ref[k, 256:, :]], axis=1)
            if i == j:
                blk = 0.5 * (blk + blk.T)
            hi, lo = split(blk)
            ghi[256*i:256*i+256, 256*j:256*j+256] = hi
            glo[256*i:256*i+256, 256*j:256*j+256] = lo
            if i != j:
                ghi[256*j:256*j+256, 256*i:256*i+256] = hi.T
                glo[256*j:256*j+256, 256*i:256*i+256] = lo.T
            k += 1
    f_ref[...] = s_ref[...]
    def body(t, _):
        bh, bl = split(f_ref[...])
        b2 = jnp.concatenate([bh, bl], axis=1)
        for i in range(4):
            r2 = dg(ghi[256*i:256*i+256, :], b2, 1, 0)
            r1 = dg(glo[256*i:256*i+256, :], bh, 1, 0)
            img[256*i:256*i+256, :] = r2[:, :128] + (r2[:, 128:] + r1)
        im = img[...]
        a_ref[...] = lax.dot_general(im, im, (((0,), (0,)), ((), ())), precision=HI, preferred_element_type=F32)
        eliminate(a_ref, q_ref, w_ref)
        f_ref[...] = lax.dot_general(img[...], w_ref[...], (((1,), (1,)), ((), ())), precision=HI, preferred_element_type=F32)
        return 0
    lax.fori_loop(0, iters, body, 0)

def k2(x, s, iters=3):
    v = pl.BlockSpec(memory_space=pltpu.VMEM)
    return pl.pallas_call(functools.partial(k2_kernel, iters=iters), out_shape=jax.ShapeDtypeStruct((1024, 128), F32),
        in_specs=[v, v], out_specs=v,
        scratch_shapes=[pltpu.VMEM((1024,1024),BF), pltpu.VMEM((1024,1024),BF), pltpu.VMEM((1024,128),F32),
                        pltpu.VMEM((128,128),F32), pltpu.VMEM((128,128),F32), pltpu.VMEM((128,128),F32)],
        compiler_params=pltpu.CompilerParams(vmem_limit_bytes=60<<20))(x, s)

def gram_kernel(u_ref, o_ref, h_ref, l_ref):
    t = pl.program_id(0)
    h, l = split(u_ref[...])
    h_ref[...] = h; l_ref[...] = l
    @pl.when(t == 0)
    def _(): o_ref[...] = jnp.zeros_like(o_ref)
    k = 0
    for i in range(4):
        for j in range(i, 4):
            hi, hj = h_ref[256*i:256*i+256, :], h_ref[256*j:256*j+256, :]
            li, lj = l_ref[256*i:256*i+256, :], l_ref[256*j:256*j+256, :]
            r = dg(hi, hj, 1, 1)
            if i == j:
                r = r + 2.0 * dg(hi, lj, 1, 1)
            else:
                r = r + (dg(hi, lj, 1, 1) + dg(li, hj, 1, 1))
            o_ref[k, :256, :] += r[:, :128]
            o_ref[k, 256:, :] += r[:, 128:]
            k += 1

def gram(u, tk=512):
    return pl.pallas_call(gram_kernel, out_shape=jax.ShapeDtypeStruct((10, 512, 128), F32),
        grid=(u.shape[1]//tk,),
        in_specs=[pl.BlockSpec((1024, tk), lambda t: (0, t))],
        out_specs=pl.BlockSpec((10, 512, 128), lambda t: (0, 0, 0)),
        scratch_shapes=[pltpu.VMEM((1024, tk), BF), pltpu.VMEM((1024, tk), BF)],
        compiler_params=pltpu.CompilerParams(vmem_limit_bytes=60<<20, dimension_semantics=("arbitrary",)))(u)

def core_kernel(f_ref, u_ref, o_ref, f2_ref):
    @pl.when(pl.program_id(0) == 0)
    def _():
        ft = f_ref[...].T
        fh, fl = split(ft)
        f2_ref[:128, :] = fh; f2_ref[128:, :] = fl
    h, l = split(u_ref[...])
    r = dg(f2_ref[...], h, 1, 0)
    o_ref[...] = r[:128, :] + (r[128:, :] + dg(f2_ref[:128, :], l, 1, 0))

def core(f, u, tk=512):
    return pl.pallas_call(core_kernel, out_shape=jax.ShapeDtypeStruct((128, u.shape[1]), F32),
        grid=(u.shape[1]//tk,),
        in_specs=[pl.BlockSpec((1024, 128), lambda t: (0, 0)), pl.BlockSpec((1024, tk), lambda t: (0, t))],
        out_specs=pl.BlockSpec((128, tk), lambda t: (0, t)),
        scratch_shapes=[pltpu.VMEM((256, 1024), BF)],
        compiler_params=pltpu.CompilerParams(vmem_limit_bytes=60<<20, dimension_semantics=("arbitrary",)))(f, u)
F32 = jnp.float32
STAGES = 5
MESH = pl.DeviceIdType.MESH

class Net:
    def __init__(self):
        self.y = lax.axis_index("grp")
        inn = lax.axis_index("in")
        self.core = lax.rem(inn, 2)
        self.x = lax.rem(inn // 2, 4)
        self.z = inn // 8
    def coord(self, axis):
        return (self.x, self.y, self.z)[axis]
    def step(self, axis, d):
        return lax.rem(self.coord(axis) + d, 4)
    def peer(self, axis, d):
        c = [self.x, self.y, self.z]
        c[axis] = self.step(axis, d)
        return (c[1], (c[2] * 4 + c[0]) * 2 + self.core)
    def twin(self):
        return (self.y, (self.z * 4 + self.x) * 2 + 1 - self.core)
    def barrier(self):
        b = pltpu.get_barrier_semaphore()
        pl.semaphore_signal(b, inc=1, device_id=self.twin(), device_id_type=MESH)
        for a in range(3):
            for d in (1, 2, 3):
                pl.semaphore_signal(b, inc=1, device_id=self.peer(a, d), device_id_type=MESH)
        pl.semaphore_wait(b, 10)

def ar_kernel(x_ref, o_ref, b0, b1, b2, b3, a0, a1, a2, ssem, rsem):
    net = Net()
    net.barrier()
    def rc(src, dst, s, k, dev):
        c = pltpu.make_async_remote_copy(src_ref=src, dst_ref=dst, send_sem=ssem.at[s, k], recv_sem=rsem.at[s, k], device_id=dev, device_id_type=MESH)
        c.start()
        return c
    sent = []
    order = [[(s + l) % 3 for l in range(3)] for s in range(STAGES)]
    m = pl.multiple_of
    cps = []
    for s in range(STAGES):
        cps.append([rc(x_ref.at[2 * s + 1 - net.core], b0.at[s], s, 0, net.twin())])
    rows = (512, 128, 32, 8)
    bufs = (b1, b2, b3)
    accs = (a0, a1, a2)
    for lvl in range(3):
        n = rows[lvl + 1]
        nxt = []
        for s in range(STAGES):
            for c in cps[s]:
                c.wait_recv()
            sent += cps[s]
            acc = accs[lvl].at[s]
            if lvl == 0:
                acc[...] = x_ref[2 * s + net.core] + b0[s]
            else:
                p = net.coord(order[s][lvl - 1])
                v = accs[lvl - 1][s, pl.ds(m(p * rows[lvl], rows[lvl]), rows[lvl]), :]
                acc[...] = v + (bufs[lvl - 1][s, 0] + (bufs[lvl - 1][s, 1] + bufs[lvl - 1][s, 2]))
            ax = order[s][lvl]
            cur = []
            for d in (1, 2, 3):
                q = net.step(ax, d)
                cur.append(rc(acc.at[pl.ds(m(q * n, n), n), :], bufs[lvl].at[s, d - 1], s, 3 * lvl + d, net.peer(ax, d)))
            nxt.append(cur)
        cps = nxt
    offs = []
    for s in range(STAGES):
        c1, c2, c3 = (net.coord(a) for a in order[s])
        offs.append((c1 * 128, c1 * 128 + c2 * 32, c1 * 128 + c2 * 32 + c3 * 8))
    for lvl in (2, 1, 0):
        n = rows[lvl + 1]
        nxt = []
        for s in range(STAGES):
            for c in cps[s]:
                c.wait_recv()
            sent += cps[s]
            unit = 2 * s + net.core
            ax = order[s][lvl]
            here = o_ref.at[unit, pl.ds(m(offs[s][lvl], n), n), :]
            if lvl == 2:
                p = net.coord(ax)
                v = a2[s, pl.ds(m(p * 8, 8), 8), :]
                here[...] = v + (b3[s, 0] + (b3[s, 1] + b3[s, 2]))
            nxt.append([rc(here, here, s, 9 + 3 * lvl + d, net.peer(ax, d)) for d in (1, 2, 3)])
        cps = nxt
    nxt = []
    for s in range(STAGES):
        for c in cps[s]:
            c.wait_recv()
        sent += cps[s]
        unit = 2 * s + net.core
        nxt.append(rc(o_ref.at[unit], o_ref.at[unit], s, 19, net.twin()))
    for c in nxt:
        c.wait_recv()
    for c in sent + nxt:
        c.wait_send()

def allreduce(x):
    v = pl.BlockSpec(memory_space=pltpu.VMEM)
    S = STAGES
    return pl.pallas_call(ar_kernel, out_shape=jax.ShapeDtypeStruct((10, 512, 128), F32),
        in_specs=[v], out_specs=v,
        scratch_shapes=[pltpu.VMEM((S, 512, 128), F32), pltpu.VMEM((S, 3, 128, 128), F32), pltpu.VMEM((S, 3, 32, 128), F32), pltpu.VMEM((S, 3, 8, 128), F32),
                        pltpu.VMEM((S, 512, 128), F32), pltpu.VMEM((S, 128, 128), F32), pltpu.VMEM((S, 32, 128), F32),
                        pltpu.SemaphoreType.DMA((S, 20)), pltpu.SemaphoreType.DMA((S, 20))],
        compiler_params=pltpu.CompilerParams(vmem_limit_bytes=60<<20, collective_id=0, has_side_effects=True))(x)


def per_device(unfolding, start_basis):
    packed = allreduce(gram(unfolding))
    factor = k2(packed, start_basis)
    return factor, core(factor, unfolding, 1024)


def solution(mesh):
    in_specs = (P(None, ("grp", "in")), P())
    out_specs = (P(), P(None, ("grp", "in")))
    return jax.shard_map(
        per_device, mesh=mesh, in_specs=in_specs, out_specs=out_specs, check_vma=False
    )
```

```python
import functools

import jax
import jax.numpy as jnp
from jax import lax
from jax.experimental import pallas as pl
from jax.experimental.pallas import tpu as pltpu
from jax.sharding import PartitionSpec as P

HI = lax.Precision.HIGHEST
F32 = jnp.float32
BF = jnp.bfloat16

def split(x):
    hi = x.astype(BF)
    return hi, (x - hi.astype(F32)).astype(BF)

def dg(a, b, ca, cb):
    return lax.dot_general(a, b, (((ca,), (cb,)), ((), ())), preferred_element_type=F32)

def eliminate(a_ref, q_ref, w_ref):
    sub = lax.broadcasted_iota(jnp.int32, (8, 128), 0)
    lane = lax.broadcasted_iota(jnp.int32, (8, 128), 1)
    M = [a_ref[8*p:8*p+8, :] for p in range(16)]
    Q = [jnp.where(lane == sub + 8*p, 1.0, 0.0).astype(F32) for p in range(16)]
    for p in range(16):
        P, R = M[p], Q[p]
        cols = [jnp.broadcast_to(P[:, 8*p+c:8*p+c+1], (8, 128)) for c in range(8)]
        piv = []
        recs = []
        for r in range(8):
            d = jnp.broadcast_to(cols[r][r:r+1, :], (8, 128))
            rec = 1.0 / d
            piv.append(d); recs.append(rec)
            if r == 7: break
            m = jnp.where(sub > r, cols[r] * rec, 0.0)
            for c in range(r+1, 8):
                cols[c] = cols[c] - m * jnp.broadcast_to(cols[c][r:r+1, :], (8, 128))
            P = P - m * jnp.broadcast_to(P[r:r+1, :], (8, 128))
            R = R - m * jnp.broadcast_to(R[r:r+1, :], (8, 128))
        dv = piv[7]; rv = recs[7]
        for r in range(7):
            dv = jnp.where(sub == r, piv[r], dv)
            rv = jnp.where(sub == r, recs[r], rv)
        w_ref[8*p:8*p+8, :] = R * (1.0 / jnp.sqrt(dv))
        if p < 15:
            T = jnp.transpose(P * rv)
            pr = [jnp.broadcast_to(P[r:r+1, :], (8, 128)) for r in range(8)]
            qr = [jnp.broadcast_to(R[r:r+1, :], (8, 128)) for r in range(8)]
            for i in range(p+1, 16):
                for r in range(8):
                    mm = jnp.broadcast_to(T[8*i:8*i+8, r:r+1], (8, 128))
                    M[i] = M[i] - mm * pr[r]
                    Q[i] = Q[i] - mm * qr[r]

def k2_kernel(x_ref, s_ref, f_ref, ghi, glo, img, a_ref, q_ref, w_ref, *, iters=3):
    k = 0
    for j in range(4):
        for i in range(j + 1):
            blk = jnp.concatenate([x_ref[k, :256, :], x_ref[k, 256:, :]], axis=1)
            if i == j:
                blk = 0.5 * (blk + blk.T)
            hi, lo = split(blk)
            ghi[256*i:256*i+256, 256*j:256*j+256] = hi
            glo[256*i:256*i+256, 256*j:256*j+256] = lo
            if i != j:
                ghi[256*j:256*j+256, 256*i:256*i+256] = hi.T
                glo[256*j:256*j+256, 256*i:256*i+256] = lo.T
            k += 1
    f_ref[...] = s_ref[...]
    def body(t, _):
        bh, bl = split(f_ref[...])
        b2 = jnp.concatenate([bh, bl], axis=1)
        for i in range(4):
            r2 = dg(ghi[256*i:256*i+256, :], b2, 1, 0)
            r1 = dg(glo[256*i:256*i+256, :], bh, 1, 0)
            img[256*i:256*i+256, :] = r2[:, :128] + (r2[:, 128:] + r1)
        im = img[...]
        a_ref[...] = lax.dot_general(im, im, (((0,), (0,)), ((), ())), precision=HI, preferred_element_type=F32)
        eliminate(a_ref, q_ref, w_ref)
        f_ref[...] = lax.dot_general(img[...], w_ref[...], (((1,), (1,)), ((), ())), precision=HI, preferred_element_type=F32)
        return 0
    lax.fori_loop(0, iters, body, 0)

def k2(x, s, iters=3):
    v = pl.BlockSpec(memory_space=pltpu.VMEM)
    return pl.pallas_call(functools.partial(k2_kernel, iters=iters), out_shape=jax.ShapeDtypeStruct((1024, 128), F32),
        in_specs=[v, v], out_specs=v,
        scratch_shapes=[pltpu.VMEM((1024,1024),BF), pltpu.VMEM((1024,1024),BF), pltpu.VMEM((1024,128),F32),
                        pltpu.VMEM((128,128),F32), pltpu.VMEM((128,128),F32), pltpu.VMEM((128,128),F32)],
        compiler_params=pltpu.CompilerParams(vmem_limit_bytes=60<<20))(x, s)

def gram_kernel(u_ref, o_ref, h_ref, l_ref):
    t = pl.program_id(0)
    h, l = split(u_ref[...])
    h_ref[...] = h; l_ref[...] = l
    @pl.when(t == 0)
    def _(): o_ref[...] = jnp.zeros_like(o_ref)
    k = 0
    for i in range(4):
        for j in range(i, 4):
            hi, hj = h_ref[256*i:256*i+256, :], h_ref[256*j:256*j+256, :]
            li, lj = l_ref[256*i:256*i+256, :], l_ref[256*j:256*j+256, :]
            r = dg(hi, hj, 1, 1)
            if i == j:
                r = r + 2.0 * dg(hi, lj, 1, 1)
            else:
                r = r + (dg(hi, lj, 1, 1) + dg(li, hj, 1, 1))
            o_ref[k, :256, :] += r[:, :128]
            o_ref[k, 256:, :] += r[:, 128:]
            k += 1

def gram(u, tk=512):
    return pl.pallas_call(gram_kernel, out_shape=jax.ShapeDtypeStruct((10, 512, 128), F32),
        grid=(u.shape[1]//tk,),
        in_specs=[pl.BlockSpec((1024, tk), lambda t: (0, t))],
        out_specs=pl.BlockSpec((10, 512, 128), lambda t: (0, 0, 0)),
        scratch_shapes=[pltpu.VMEM((1024, tk), BF), pltpu.VMEM((1024, tk), BF)],
        compiler_params=pltpu.CompilerParams(vmem_limit_bytes=60<<20, dimension_semantics=("arbitrary",)))(u)

def core_kernel(f_ref, u_ref, o_ref, f2_ref):
    @pl.when(pl.program_id(0) == 0)
    def _():
        ft = f_ref[...].T
        fh, fl = split(ft)
        f2_ref[:128, :] = fh; f2_ref[128:, :] = fl
    h, l = split(u_ref[...])
    r = dg(f2_ref[...], h, 1, 0)
    o_ref[...] = r[:128, :] + (r[128:, :] + dg(f2_ref[:128, :], l, 1, 0))

def core(f, u, tk=512):
    return pl.pallas_call(core_kernel, out_shape=jax.ShapeDtypeStruct((128, u.shape[1]), F32),
        grid=(u.shape[1]//tk,),
        in_specs=[pl.BlockSpec((1024, 128), lambda t: (0, 0)), pl.BlockSpec((1024, tk), lambda t: (0, t))],
        out_specs=pl.BlockSpec((128, tk), lambda t: (0, t)),
        scratch_shapes=[pltpu.VMEM((256, 1024), BF)],
        compiler_params=pltpu.CompilerParams(vmem_limit_bytes=60<<20, dimension_semantics=("arbitrary",)))(f, u)

MESH = pl.DeviceIdType.MESH
BLOCKS = [(i, j) for j in range(4) for i in range(j + 1)]
STAGES = ((0, 3), (3, 6), (6, 8), (8, 9), (9, 10))
KH = 2048
TICKS = [(0, 0), (0, 1), (1, 0), (1, 1), (2, 0), (2, 1)] + [(k, h) for k in range(3, 10) for h in range(2)]


class Net:
    def __init__(self):
        self.y = lax.axis_index("grp")
        self.inn = lax.axis_index("in")
        self.core = lax.rem(self.inn, 2)
        self.x = lax.rem(self.inn // 2, 4)
        self.z = self.inn // 8

    def axis(self, number):
        a = lax.rem(number, 3)
        ex, ey, ez = (2 - a) * (1 - a) // 2, a * (2 - a), a * (a - 1) // 2
        return Axis(self, ex, ey, ez)

    def twin(self):
        return (self.y, self.inn + 1 - 2 * self.core)

    def barrier(self):
        b = pltpu.get_barrier_semaphore()
        pl.semaphore_signal(b, inc=1, device_id=self.twin(), device_id_type=MESH)
        for e in ((1, 0, 0), (0, 1, 0), (0, 0, 1)):
            for d in (1, 2, 3):
                pl.semaphore_signal(b, inc=1, device_id=Axis(self, *e).peer(d), device_id_type=MESH)
        pl.semaphore_wait(b, 10)


class Axis:
    def __init__(self, net, ex, ey, ez):
        self.net, self.e = net, (ex, ey, ez)
        self.me = net.x * ex + net.y * ey + net.z * ez

    def at(self, d):
        return lax.rem(self.me + d, 4)

    def peer(self, d):
        ex, ey, ez = self.e
        delta = self.at(d) - self.me
        return (self.net.y + delta * ey, self.net.inn + delta * (2 * ex + 8 * ez))


def rows(start, n):
    return pl.ds(pl.multiple_of(start, n), n)


class Reduce:
    def __init__(self, net, x, o, b0, a0, b1, a1, b2, a2, b3, ssem, rsem):
        self.net, self.x, self.o = net, x, o
        self.b0, self.a0, self.b1, self.a1, self.b2, self.a2, self.b3 = b0, a0, b1, a1, b2, a2, b3
        self.ssem, self.rsem = ssem, rsem
        self.flying, self.sent = {}, []
        self.axes = {}
        base = [net.axis(2 * net.core + e) for e in range(3)]
        for s in range(len(STAGES)):
            for p in range(2):
                self.axes[s, p] = [base[(s + p + lvl) % 3] for lvl in range(3)]

    def send(self, src, dst, s, k, dev):
        c = pltpu.make_async_remote_copy(
            src_ref=src, dst_ref=dst, send_sem=self.ssem.at[s, k], recv_sem=self.rsem.at[s, k],
            device_id=dev, device_id_type=MESH,
        )
        c.start()
        self.flying.setdefault(s, []).append(c)

    def land(self, s):
        for c in self.flying.get(s, []):
            c.wait_recv()
        self.sent += self.flying.get(s, [])
        self.flying[s] = []

    def step(self, s, phase):
        u = slice(*STAGES[s])
        core = self.net.core
        self.land(s)
        if phase == 0:
            self.send(self.x.at[u, rows(256 - 256 * core, 256), :], self.b0.at[u], s, 0, self.net.twin())
            return
        if phase == 7:
            half = self.o.at[u, rows(256 * core, 256), :]
            self.send(half, half, s, 31, self.net.twin())
            return
        if phase == 8:
            return
        if phase == 1:
            self.a0[u] = self.x[u, rows(256 * core, 256), :] + self.b0[u]
        for p in range(2):
            x1, x2, x3 = self.axes[s, p]
            if phase == 1:
                for d in (1, 2, 3):
                    src = self.a0.at[u, rows(128 * p + 32 * x1.at(d), 32), :]
                    self.send(src, self.b1.at[p, d - 1, u], s, 1 + 15 * p + d - 1, x1.peer(d))
            if phase == 2:
                own = self.a0[u, rows(128 * p + 32 * x1.me, 32), :]
                self.a1[p, u] = own + (self.b1[p, 0, u] + (self.b1[p, 1, u] + self.b1[p, 2, u]))
                for d in (1, 2, 3):
                    src = self.a1.at[p, u, rows(8 * x2.at(d), 8), :]
                    self.send(src, self.b2.at[p, d - 1, u], s, 4 + 15 * p + d - 1, x2.peer(d))
            if phase == 3:
                own = self.a1[p, u, rows(8 * x2.me, 8), :]
                self.a2[p, u] = own + (self.b2[p, 0, u] + (self.b2[p, 1, u] + self.b2[p, 2, u]))
                for d in (1, 2, 3):
                    self.send(self.a2.at[p, u], self.b3.at[p, d - 1, u], s, 7 + 15 * p + d - 1, x3.peer(d))
            if phase == 4:
                here = self.o.at[u, rows(256 * core + 128 * p + 32 * x1.me + 8 * x2.me, 8), :]
                here[...] = self.ordered(p, u, x3)
                for d in (1, 2, 3):
                    self.send(here, here, s, 10 + 15 * p + d - 1, x2.peer(d))
            if phase == 5:
                here = self.o.at[u, rows(256 * core + 128 * p + 32 * x1.me, 32), :]
                for d in (1, 2, 3):
                    self.send(here, here, s, 13 + 15 * p + d - 1, x1.peer(d))

    def ordered(self, p, u, axis):
        own, t1, t2, t3 = self.a2[p, u], self.b3[p, 0, u], self.b3[p, 1, u], self.b3[p, 2, u]
        even = lax.rem(axis.me, 2) == 0
        near = jnp.where(even, t3, t1)
        far = jnp.where(even, t1, t3)
        return (own + near) + (t2 + far)


def plan(ticks):
    ev = []
    for s, (a, b) in enumerate(STAGES):
        m = b - a
        t = max(w for k, _, w in ticks if k < b)
        cost = [1.0 + 0.3 * m, 2.2 + 0.85 * m, 2.2 + 0.2 * m, 2.2 + 0.2 * m, 2.2 + 0.2 * m, 2.2 + 0.85 * m, 0.0, 1.0 + 0.3 * m, 0.0]
        for ph in (0, 1, 2, 3, 4, 5, 7, 8):
            ev.append((t, s, ph))
            t += cost[ph]
    ev.sort()
    return ev


def gram_reduce_kernel(u_hbm, o_ref, stg, hl, x, b0, a0, b1, a1, b2, a2, b3, lsem, ssem, rsem, *, comm=True):
    def load(n):
        i, h = divmod(n, 2)
        return pltpu.make_async_copy(
            u_hbm.at[256 * i:256 * i + 256, KH * h:KH * h + KH], stg.at[n % 4], lsem.at[n % 4]
        )
    for n in range(4):
        load(n).start()
    if comm:
        net = Net()
        net.barrier()
        red = Reduce(net, x, o_ref, b0, a0, b1, a1, b2, a2, b3, ssem, rsem)

    def convert(n):
        i, h = divmod(n, 2)
        for c in range(0, KH, 256):
            hi, lo = split(stg[n % 4, :, c:c + 256])
            hl[i, :256, KH * h + c:KH * h + c + 256] = hi
            hl[i, 256:, KH * h + c:KH * h + c + 256] = lo

    ticks, t = [], 3.0
    for n, (k, h) in enumerate(TICKS):
        i, j = BLOCKS[k]
        t += 0.275 * (2 if i == j else 3) + (0.8 if n < 7 else 0.0)
        ticks.append((k, h, t))
    events = plan(ticks) if comm else []
    load(0).wait()
    convert(0)
    done = 1
    for n, (k, h, t) in enumerate(ticks):
        i, j = BLOCKS[k]
        if done < 8:
            if done >= 1 and done + 3 < 8:
                load(done + 3).start()
            load(done).wait()
            convert(done)
            done += 1
        ks = slice(KH * h, KH * h + KH)
        if i == j:
            r = dg(hl[i, :256, ks], hl[j, :256, ks], 1, 1) + 2.0 * dg(hl[i, :256, ks], hl[j, 256:, ks], 1, 1)
        else:
            r2 = dg(hl[i, :, ks], hl[j, :256, ks], 1, 1)
            r = r2[:256] + (r2[256:] + dg(hl[i, :256, ks], hl[j, 256:, ks], 1, 1))
        dst = x if comm else o_ref
        if h == 0:
            dst[k, :256, :] = r[:, :128]
            dst[k, 256:, :] = r[:, 128:]
        else:
            dst[k, :256, :] += r[:, :128]
            dst[k, 256:, :] += r[:, 128:]
        while events and events[0][0] <= t:
            _, s, ph = events.pop(0)
            red.step(s, ph)
    for _, s, ph in events:
        red.step(s, ph)
    if comm:
        for c in red.sent:
            c.wait_send()


def gram_reduce(u, comm=True):
    v = pl.BlockSpec(memory_space=pltpu.VMEM)
    n = len(STAGES)
    V = pltpu.VMEM
    kw = dict(collective_id=0, has_side_effects=True) if comm else {}
    return pl.pallas_call(
        functools.partial(gram_reduce_kernel, comm=comm),
        out_shape=jax.ShapeDtypeStruct((10, 512, 128), F32),
        in_specs=[pl.BlockSpec(memory_space=pl.ANY)], out_specs=v,
        scratch_shapes=[
            V((4, 256, KH), F32), V((4, 512, 2 * KH), BF), V((10, 512, 128), F32),
            V((10, 256, 128), F32), V((10, 256, 128), F32),
            V((2, 3, 10, 32, 128), F32), V((2, 10, 32, 128), F32),
            V((2, 3, 10, 8, 128), F32), V((2, 10, 8, 128), F32), V((2, 3, 10, 8, 128), F32),
            pltpu.SemaphoreType.DMA((4,)), pltpu.SemaphoreType.DMA((n, 32)), pltpu.SemaphoreType.DMA((n, 32)),
        ],
        compiler_params=pltpu.CompilerParams(vmem_limit_bytes=60 << 20, **kw),
    )(u)


def per_device(unfolding, start_basis):
    packed = gram_reduce(unfolding)
    factor = k2(packed, start_basis)
    return factor, core(factor, unfolding, 1024)


def solution(mesh):
    in_specs = (P(None, ("grp", "in")), P())
    out_specs = (P(), P(None, ("grp", "in")))
    return jax.shard_map(
        per_device, mesh=mesh, in_specs=in_specs, out_specs=out_specs, check_vma=False
    )
```

```python
import functools

import jax
import jax.numpy as jnp
from jax import lax
from jax.experimental import pallas as pl
from jax.experimental.pallas import tpu as pltpu
from jax.sharding import PartitionSpec as P

HI = lax.Precision.HIGHEST
F32 = jnp.float32
BF = jnp.bfloat16

def split(x):
    hi = x.astype(BF)
    return hi, (x - hi.astype(F32)).astype(BF)

def dg(a, b, ca, cb):
    return lax.dot_general(a, b, (((ca,), (cb,)), ((), ())), preferred_element_type=F32)

GROUP = 8


def eliminate(a_ref, q_ref, w_ref):
    sub = lax.broadcasted_iota(jnp.int32, (8, 128), 0)
    lane = lax.broadcasted_iota(jnp.int32, (8, 128), 1)
    wide = lambda v: jnp.broadcast_to(v, (8, 128))
    row = lambda v, r: wide(v[r:r + 1, :])
    col = lambda v, c: wide(v[:, c:c + 1])
    M = [a_ref[8 * p:8 * p + 8, :] for p in range(16)]
    on = [lane == sub + 8 * p for p in range(16)]
    diag = jnp.where(on[0], M[0], 0.0)
    for p in range(1, 16):
        diag = diag + jnp.where(on[p], M[p], 0.0)
    scale = wide(1.0 / jnp.sqrt(jnp.sum(diag, axis=0, keepdims=True)))
    Q = [jnp.where(on[p], scale, 0.0) for p in range(16)]
    for p in range(16):
        M[p] = M[p] * scale * wide(jnp.sum(Q[p], axis=1, keepdims=True))
    done = []
    for p in range(16):
        P, R = M[p], Q[p]
        last = p == 15
        edge = p % GROUP == GROUP - 1
        N, S = (None, None) if edge else (M[p + 1], Q[p + 1])
        cs = [col(P, 8 * p + c) for c in range(8)] if p % GROUP == 0 else gs
        es, fs, gs = [], [], []
        if not edge:
            es = [col(N, 8 * p + c) for c in range(8)]
            fs = [col(P, 8 * p + 8 + c) for c in range(8)]
            gs = [col(N, 8 * p + 8 + c) for c in range(8)]
        dv = rv = tv = jnp.zeros((8, 128), F32)
        for r in range(0, 8, 2):
            a, b, d = row(cs[r], r), row(cs[r], r + 1), row(cs[r + 1], r + 1)
            det = a * d - b * b
            rdet = 1.0 / det
            ra = 1.0 / a
            dv = jnp.where(sub == r, a, jnp.where(sub == r + 1, det * ra, dv))
            rv = jnp.where(sub == r, ra, jnp.where(sub == r + 1, a * rdet, rv))
            tv = jnp.where(sub == r + 1, b * ra, tv)
            sets = []
            if r < 6:
                below = sub > r + 1
                sets.append((jnp.where(below, d * cs[r] - b * cs[r + 1], 0.0),
                             jnp.where(below, a * cs[r + 1] - b * cs[r], 0.0)))
            if not edge:
                sets.append((d * es[r] - b * es[r + 1], a * es[r + 1] - b * es[r]))
            p0, p1, q0, q1 = row(P, r), row(P, r + 1), row(R, r), row(R, r + 1)
            for k in range(r + 2, 8):
                s0, s1 = row(cs[k], r), row(cs[k], r + 1)
                if not edge:
                    n0, n1 = sets[-1]
                    es[k] = es[k] - rdet * (n0 * s0 + n1 * s1)
                n0, n1 = sets[0]
                cs[k] = cs[k] - rdet * (n0 * s0 + n1 * s1)
            for k in range(8 if not edge else 0):
                s0, s1 = row(fs[k], r), row(fs[k], r + 1)
                n0, n1 = sets[-1]
                gs[k] = gs[k] - rdet * (n0 * s0 + n1 * s1)
                if r < 6:
                    n0, n1 = sets[0]
                    fs[k] = fs[k] - rdet * (n0 * s0 + n1 * s1)
            if r < 6:
                n0, n1 = sets[0]
                P = P - rdet * (n0 * p0 + n1 * p1)
                R = R - rdet * (n0 * q0 + n1 * q1)
            if not edge:
                n0, n1 = sets[-1]
                N = N - rdet * (n0 * p0 + n1 * p1)
                S = S - rdet * (n0 * q0 + n1 * q1)
        P = P - tv * pltpu.roll(P, 1, 0)
        R = R - tv * pltpu.roll(R, 1, 0)
        w_ref[8 * p:8 * p + 8, :] = R * (1.0 / jnp.sqrt(dv))
        if not edge:
            M[p + 1], Q[p + 1] = N, S
        done.append((P, R, P * rv))
        group = p // GROUP
        stop = GROUP * group + GROUP
        if p + 2 < min(stop, 16):
            T = jnp.transpose(P * rv)
            pr = [row(P, r) for r in range(8)]
            qr = [row(R, r) for r in range(8)]
            for i in range(p + 2, stop):
                for r in range(8):
                    mm = wide(T[8 * i:8 * i + 8, r:r + 1])
                    M[i] = M[i] - mm * pr[r]
                    Q[i] = Q[i] - mm * qr[r]
        if p == stop - 1 and not last:
            parts = done[GROUP * group:]
            left = jnp.concatenate([v[2] for v in parts], axis=0)
            right = jnp.concatenate([jnp.concatenate(v[:2], axis=1) for v in parts], axis=0)
            upd = lax.dot_general(left, right, (((0,), (0,)), ((), ())), precision=HI, preferred_element_type=F32)
            for i in range(stop, 16):
                M[i] = M[i] - upd[8 * i:8 * i + 8, :128]
                Q[i] = Q[i] - upd[8 * i:8 * i + 8, 128:]


ITERS = 3


def tail_kernel(x_ref, s_ref, u_hbm, f_ref, o_hbm, ghi, glo, img, a_ref, q_ref, w_ref, u_ref, f2, out, lsem, osem):
    pieces = [slice(c, c + 512) for c in range(0, 4096, 512)]
    loads = [pltpu.make_async_copy(u_hbm.at[:, c], u_ref.at[:, c], lsem.at[n]) for n, c in enumerate(pieces)]
    for c in loads:
        c.start()
    k = 0
    for j in range(4):
        for i in range(j + 1):
            blk = jnp.concatenate([x_ref[k, :256, :], x_ref[k, 256:, :]], axis=1)
            if i == j:
                blk = 0.5 * (blk + blk.T)
            hi, lo = split(blk)
            ghi[256*i:256*i+256, 256*j:256*j+256] = hi
            glo[256*i:256*i+256, 256*j:256*j+256] = lo
            if i != j:
                ghi[256*j:256*j+256, 256*i:256*i+256] = hi.T
                glo[256*j:256*j+256, 256*i:256*i+256] = lo.T
            k += 1
    f_ref[...] = s_ref[...]

    def body(t, _):
        bh, bl = split(f_ref[...])
        b2 = jnp.concatenate([bh, bl], axis=1)
        for i in range(4):
            r2 = dg(ghi[256*i:256*i+256, :], b2, 1, 0)
            r1 = dg(glo[256*i:256*i+256, :], bh, 1, 0)
            img[256*i:256*i+256, :] = r2[:, :128] + (r2[:, 128:] + r1)
        im = img[...]
        a_ref[...] = lax.dot_general(im, im, (((0,), (0,)), ((), ())), precision=HI, preferred_element_type=F32)
        eliminate(a_ref, q_ref, w_ref)
        f_ref[...] = lax.dot_general(img[...], w_ref[...], (((1,), (1,)), ((), ())), precision=HI, preferred_element_type=F32)
        return 0

    lax.fori_loop(0, ITERS, body, 0)
    fh, fl = split(f_ref[...].T)
    f2[:128, :] = fh
    f2[128:, :] = fl
    for c in loads:
        c.wait()
    stores = []
    for n, c in enumerate(pieces):
        h, l = split(u_ref[:, c])
        r = dg(f2[...], h, 1, 0)
        out[:, c] = r[:128, :] + (r[128:, :] + dg(f2[:128, :], l, 1, 0))
        if n % 2 == 1:
            two = slice(c.stop - 1024, c.stop)
            stores.append(pltpu.make_async_copy(out.at[:, two], o_hbm.at[:, two], osem.at[n // 2]))
            stores[-1].start()
    for c in stores:
        c.wait()


def iterate_project(x, s, u):
    v, anyw = pl.BlockSpec(memory_space=pltpu.VMEM), pl.BlockSpec(memory_space=pl.ANY)
    V = pltpu.VMEM
    return pl.pallas_call(
        tail_kernel,
        out_shape=(jax.ShapeDtypeStruct((1024, 128), F32), jax.ShapeDtypeStruct((128, 4096), F32)),
        in_specs=[v, v, anyw], out_specs=(v, anyw),
        scratch_shapes=[V((1024, 1024), BF), V((1024, 1024), BF), V((1024, 128), F32),
                        V((128, 128), F32), V((128, 128), F32), V((128, 128), F32),
                        V((1024, 4096), F32), V((256, 1024), BF), V((128, 4096), F32),
                        pltpu.SemaphoreType.DMA((8,)), pltpu.SemaphoreType.DMA((4,))],
        compiler_params=pltpu.CompilerParams(vmem_limit_bytes=60 << 20),
    )(x, s, u)

MESH = pl.DeviceIdType.MESH
BLOCKS = [(i, j) for j in range(4) for i in range(j + 1)]
STAGES = ((0, 3), (3, 6), (6, 8), (8, 9), (9, 10))
KH = 2048
LAT = (2.0, 3.9, 3.0)
TICKS = [(0, 0), (0, 1), (1, 0), (1, 1), (2, 0), (2, 1)] + [(k, h) for k in range(3, 10) for h in range(2)]


class Net:
    def __init__(self):
        self.y = lax.axis_index("grp")
        self.inn = lax.axis_index("in")
        self.core = lax.rem(self.inn, 2)
        self.x = lax.rem(self.inn // 2, 4)
        self.z = self.inn // 8

    def axis(self, number):
        a = lax.rem(number, 3)
        ex, ey, ez = (2 - a) * (1 - a) // 2, a * (2 - a), a * (a - 1) // 2
        return Axis(self, ex, ey, ez)

    def twin(self):
        return (self.y, self.inn + 1 - 2 * self.core)

    def barrier(self):
        b = pltpu.get_barrier_semaphore()
        pl.semaphore_signal(b, inc=1, device_id=self.twin(), device_id_type=MESH)
        for e in ((1, 0, 0), (0, 1, 0), (0, 0, 1)):
            for d in (1, 2, 3):
                pl.semaphore_signal(b, inc=1, device_id=Axis(self, *e).peer(d), device_id_type=MESH)
        pl.semaphore_wait(b, 10)


class Axis:
    def __init__(self, net, ex, ey, ez):
        self.net, self.e = net, (ex, ey, ez)
        self.me = net.x * ex + net.y * ey + net.z * ez

    def at(self, d):
        return lax.rem(self.me + d, 4)

    def peer(self, d):
        ex, ey, ez = self.e
        delta = self.at(d) - self.me
        return (self.net.y + delta * ey, self.net.inn + delta * (2 * ex + 8 * ez))


def rows(start, n):
    return pl.ds(pl.multiple_of(start, n), n)


class Reduce:
    def __init__(self, net, x, o, b0, a0, b1, a1, b2, a2, b3, ssem, rsem):
        self.net, self.x, self.o = net, x, o
        self.b0, self.a0, self.b1, self.a1, self.b2, self.a2, self.b3 = b0, a0, b1, a1, b2, a2, b3
        self.ssem, self.rsem = ssem, rsem
        self.flying, self.sent = {}, []
        self.axes = {}
        base = [net.axis(2 * net.core + e) for e in range(3)]
        for s in range(len(STAGES)):
            for p in range(2):
                self.axes[s, p] = [base[(s + p + lvl) % 3] for lvl in range(3)]

    def send(self, src, dst, s, k, dev):
        c = pltpu.make_async_remote_copy(
            src_ref=src, dst_ref=dst, send_sem=self.ssem.at[s, k], recv_sem=self.rsem.at[s, k],
            device_id=dev, device_id_type=MESH,
        )
        c.start()
        self.flying.setdefault(s, []).append(c)

    def land(self, s):
        for c in self.flying.get(s, []):
            c.wait_recv()
        self.sent += self.flying.get(s, [])
        self.flying[s] = []

    def step(self, s, phase):
        u = slice(*STAGES[s])
        core = self.net.core
        self.land(s)
        if phase == 0:
            self.send(self.x.at[u, rows(256 - 256 * core, 256), :], self.b0.at[u], s, 0, self.net.twin())
            return
        if phase == 7:
            half = self.o.at[u, rows(256 * core, 256), :]
            self.send(half, half, s, 31, self.net.twin())
            return
        if phase == 8:
            return
        if phase == 1:
            self.a0[u] = self.x[u, rows(256 * core, 256), :] + self.b0[u]
        for p in range(2):
            x1, x2, x3 = self.axes[s, p]
            if phase == 1:
                for d in (1, 2, 3):
                    src = self.a0.at[u, rows(128 * p + 32 * x1.at(d), 32), :]
                    self.send(src, self.b1.at[p, d - 1, u], s, 1 + 15 * p + d - 1, x1.peer(d))
            if phase == 2:
                own = self.a0[u, rows(128 * p + 32 * x1.me, 32), :]
                self.a1[p, u] = own + (self.b1[p, 0, u] + (self.b1[p, 1, u] + self.b1[p, 2, u]))
                for d in (1, 2, 3):
                    src = self.a1.at[p, u, rows(8 * x2.at(d), 8), :]
                    self.send(src, self.b2.at[p, d - 1, u], s, 4 + 15 * p + d - 1, x2.peer(d))
            if phase == 3:
                own = self.a1[p, u, rows(8 * x2.me, 8), :]
                self.a2[p, u] = own + (self.b2[p, 0, u] + (self.b2[p, 1, u] + self.b2[p, 2, u]))
                for d in (1, 2, 3):
                    self.send(self.a2.at[p, u], self.b3.at[p, d - 1, u], s, 7 + 15 * p + d - 1, x3.peer(d))
            if phase == 4:
                here = self.o.at[u, rows(256 * core + 128 * p + 32 * x1.me + 8 * x2.me, 8), :]
                here[...] = self.ordered(p, u, x3)
                for d in (1, 2, 3):
                    self.send(here, here, s, 10 + 15 * p + d - 1, x2.peer(d))
            if phase == 5:
                here = self.o.at[u, rows(256 * core + 128 * p + 32 * x1.me, 32), :]
                for d in (1, 2, 3):
                    self.send(here, here, s, 13 + 15 * p + d - 1, x1.peer(d))

    def ordered(self, p, u, axis):
        own, t1, t2, t3 = self.a2[p, u], self.b3[p, 0, u], self.b3[p, 1, u], self.b3[p, 2, u]
        even = lax.rem(axis.me, 2) == 0
        near = jnp.where(even, t3, t1)
        far = jnp.where(even, t1, t3)
        return (own + near) + (t2 + far)


def plan(ticks):
    ev = []
    for s, (a, b) in enumerate(STAGES):
        m = b - a
        t = max(w for k, _, w in ticks if k < b)
        cost = [LAT[0] + 0.3 * m, LAT[1] + 0.85 * m, LAT[1] + 0.25 * m, LAT[2] + 0.25 * m, LAT[1] + 0.25 * m, LAT[1] + 0.85 * m, 0.0, LAT[0] + 0.3 * m, 0.0]
        for ph in (0, 1, 2, 3, 4, 5, 7, 8):
            ev.append((t, s, ph))
            t += cost[ph]
    ev.sort()
    return ev


def gram_reduce_kernel(u_hbm, o_ref, stg, hl, x, b0, a0, b1, a1, b2, a2, b3, lsem, ssem, rsem, *, comm=True):
    def load(n):
        i, h = divmod(n, 2)
        return pltpu.make_async_copy(
            u_hbm.at[256 * i:256 * i + 256, KH * h:KH * h + KH], stg.at[n % 4], lsem.at[n % 4]
        )
    for n in range(4):
        load(n).start()
    if comm:
        net = Net()
        net.barrier()
        red = Reduce(net, x, o_ref, b0, a0, b1, a1, b2, a2, b3, ssem, rsem)

    def convert(n):
        i, h = divmod(n, 2)
        for c in range(0, KH, 256):
            hi, lo = split(stg[n % 4, :, c:c + 256])
            hl[i, :256, KH * h + c:KH * h + c + 256] = hi
            hl[i, 256:, KH * h + c:KH * h + c + 256] = lo

    ticks, t = [], 3.0
    for n, (k, h) in enumerate(TICKS):
        i, j = BLOCKS[k]
        t += 0.275 * (2 if i == j else 3) + (0.8 if n < 7 else 0.0)
        ticks.append((k, h, t))
    events = plan(ticks) if comm else []
    load(0).wait()
    convert(0)
    done = 1
    for n, (k, h, t) in enumerate(ticks):
        i, j = BLOCKS[k]
        if done < 8:
            if done >= 1 and done + 3 < 8:
                load(done + 3).start()
            load(done).wait()
            convert(done)
            done += 1
        ks = slice(KH * h, KH * h + KH)
        if i == j:
            r = dg(hl[i, :256, ks], hl[j, :256, ks], 1, 1) + 2.0 * dg(hl[i, :256, ks], hl[j, 256:, ks], 1, 1)
        else:
            r2 = dg(hl[i, :, ks], hl[j, :256, ks], 1, 1)
            r = r2[:256] + (r2[256:] + dg(hl[i, :256, ks], hl[j, 256:, ks], 1, 1))
        dst = x if comm else o_ref
        if h == 0:
            dst[k, :256, :] = r[:, :128]
            dst[k, 256:, :] = r[:, 128:]
        else:
            dst[k, :256, :] += r[:, :128]
            dst[k, 256:, :] += r[:, 128:]
        while events and events[0][0] <= t:
            _, s, ph = events.pop(0)
            red.step(s, ph)
    for _, s, ph in events:
        red.step(s, ph)
    if comm:
        for c in red.sent:
            c.wait_send()


def gram_reduce(u, comm=True):
    v = pl.BlockSpec(memory_space=pltpu.VMEM)
    n = len(STAGES)
    V = pltpu.VMEM
    kw = dict(collective_id=0, has_side_effects=True) if comm else {}
    return pl.pallas_call(
        functools.partial(gram_reduce_kernel, comm=comm),
        out_shape=jax.ShapeDtypeStruct((10, 512, 128), F32),
        in_specs=[pl.BlockSpec(memory_space=pl.ANY)], out_specs=v,
        scratch_shapes=[
            V((4, 256, KH), F32), V((4, 512, 2 * KH), BF), V((10, 512, 128), F32),
            V((10, 256, 128), F32), V((10, 256, 128), F32),
            V((2, 3, 10, 32, 128), F32), V((2, 10, 32, 128), F32),
            V((2, 3, 10, 8, 128), F32), V((2, 10, 8, 128), F32), V((2, 3, 10, 8, 128), F32),
            pltpu.SemaphoreType.DMA((4,)), pltpu.SemaphoreType.DMA((n, 32)), pltpu.SemaphoreType.DMA((n, 32)),
        ],
        compiler_params=pltpu.CompilerParams(vmem_limit_bytes=60 << 20, **kw),
    )(u)


def per_device(unfolding, start_basis):
    packed = gram_reduce(unfolding)
    return iterate_project(packed, start_basis, unfolding)


def solution(mesh):
    in_specs = (P(None, ("grp", "in")), P())
    out_specs = (P(), P(None, ("grp", "in")))
    return jax.shard_map(
        per_device, mesh=mesh, in_specs=in_specs, out_specs=out_specs, check_vma=False
    )
```

```python
import functools

import jax
import jax.numpy as jnp
from jax import lax
from jax.experimental import pallas as pl
from jax.experimental.pallas import tpu as pltpu
from jax.sharding import PartitionSpec as P

HI = lax.Precision.HIGHEST
F32 = jnp.float32
BF = jnp.bfloat16

def split(x):
    hi = x.astype(BF)
    return hi, (x - hi.astype(F32)).astype(BF)

def dg(a, b, ca, cb):
    return lax.dot_general(a, b, (((ca,), (cb,)), ((), ())), preferred_element_type=F32)

GROUP = 8


def eliminate(a_ref, q_ref, w_ref):
    sub = lax.broadcasted_iota(jnp.int32, (8, 128), 0)
    lane = lax.broadcasted_iota(jnp.int32, (8, 128), 1)
    wide = lambda v: jnp.broadcast_to(v, (8, 128))
    row = lambda v, r: wide(v[r:r + 1, :])
    col = lambda v, c: wide(v[:, c:c + 1])
    M = [a_ref[8 * p:8 * p + 8, :] for p in range(16)]
    on = [lane == sub + 8 * p for p in range(16)]
    diag = jnp.where(on[0], M[0], 0.0)
    for p in range(1, 16):
        diag = diag + jnp.where(on[p], M[p], 0.0)
    scale = wide(1.0 / jnp.sqrt(jnp.sum(diag, axis=0, keepdims=True)))
    Q = [jnp.where(on[p], scale, 0.0) for p in range(16)]
    for p in range(16):
        M[p] = M[p] * scale * wide(jnp.sum(Q[p], axis=1, keepdims=True))
    done = []
    for p in range(16):
        P, R = M[p], Q[p]
        last = p == 15
        edge = p % GROUP == GROUP - 1
        N, S = (None, None) if edge else (M[p + 1], Q[p + 1])
        cs = [col(P, 8 * p + c) for c in range(8)] if p % GROUP == 0 else gs
        es, fs, gs = [], [], []
        if not edge:
            es = [col(N, 8 * p + c) for c in range(8)]
            fs = [col(P, 8 * p + 8 + c) for c in range(8)]
            gs = [col(N, 8 * p + 8 + c) for c in range(8)]
        dv = rv = tv = jnp.zeros((8, 128), F32)
        for r in range(0, 8, 2):
            a, b, d = row(cs[r], r), row(cs[r], r + 1), row(cs[r + 1], r + 1)
            det = a * d - b * b
            rdet = 1.0 / det
            ra = 1.0 / a
            dv = jnp.where(sub == r, a, jnp.where(sub == r + 1, det * ra, dv))
            rv = jnp.where(sub == r, ra, jnp.where(sub == r + 1, a * rdet, rv))
            tv = jnp.where(sub == r + 1, b * ra, tv)
            sets = []
            if r < 6:
                below = sub > r + 1
                sets.append((jnp.where(below, d * cs[r] - b * cs[r + 1], 0.0),
                             jnp.where(below, a * cs[r + 1] - b * cs[r], 0.0)))
            if not edge:
                sets.append((d * es[r] - b * es[r + 1], a * es[r + 1] - b * es[r]))
            p0, p1, q0, q1 = row(P, r), row(P, r + 1), row(R, r), row(R, r + 1)
            for k in range(r + 2, 8):
                s0, s1 = row(cs[k], r), row(cs[k], r + 1)
                if not edge:
                    n0, n1 = sets[-1]
                    es[k] = es[k] - rdet * (n0 * s0 + n1 * s1)
                n0, n1 = sets[0]
                cs[k] = cs[k] - rdet * (n0 * s0 + n1 * s1)
            for k in range(8 if not edge else 0):
                s0, s1 = row(fs[k], r), row(fs[k], r + 1)
                n0, n1 = sets[-1]
                gs[k] = gs[k] - rdet * (n0 * s0 + n1 * s1)
                if r < 6:
                    n0, n1 = sets[0]
                    fs[k] = fs[k] - rdet * (n0 * s0 + n1 * s1)
            if r < 6:
                n0, n1 = sets[0]
                P = P - rdet * (n0 * p0 + n1 * p1)
                R = R - rdet * (n0 * q0 + n1 * q1)
            if not edge:
                n0, n1 = sets[-1]
                N = N - rdet * (n0 * p0 + n1 * p1)
                S = S - rdet * (n0 * q0 + n1 * q1)
        P = P - tv * pltpu.roll(P, 1, 0)
        R = R - tv * pltpu.roll(R, 1, 0)
        w_ref[8 * p:8 * p + 8, :] = R * (1.0 / jnp.sqrt(dv))
        if not edge:
            M[p + 1], Q[p + 1] = N, S
        done.append((P, R, P * rv))
        group = p // GROUP
        stop = GROUP * group + GROUP
        if p + 2 < min(stop, 16):
            T = jnp.transpose(P * rv)
            pr = [row(P, r) for r in range(8)]
            qr = [row(R, r) for r in range(8)]
            for i in range(p + 2, stop):
                for r in range(8):
                    mm = wide(T[8 * i:8 * i + 8, r:r + 1])
                    M[i] = M[i] - mm * pr[r]
                    Q[i] = Q[i] - mm * qr[r]
        if p == stop - 1 and not last:
            parts = done[GROUP * group:]
            left = jnp.concatenate([v[2] for v in parts], axis=0)
            right = jnp.concatenate([jnp.concatenate(v[:2], axis=1) for v in parts], axis=0)
            upd = lax.dot_general(left, right, (((0,), (0,)), ((), ())), precision=HI, preferred_element_type=F32)
            for i in range(stop, 16):
                M[i] = M[i] - upd[8 * i:8 * i + 8, :128]
                Q[i] = Q[i] - upd[8 * i:8 * i + 8, 128:]


ITERS = 3


def tail_kernel(x_ref, s_ref, u_hbm, f_ref, o_hbm, ghi, glo, img, a_ref, q_ref, w_ref, u_ref, f2, out, lsem, osem):
    pieces = [slice(c, c + 512) for c in range(0, 4096, 512)]
    loads = [pltpu.make_async_copy(u_hbm.at[:, c], u_ref.at[:, c], lsem.at[n]) for n, c in enumerate(pieces)]
    for c in loads:
        c.start()
    k = 0
    for j in range(4):
        for i in range(j + 1):
            blk = jnp.concatenate([x_ref[k, :256, :], x_ref[k, 256:, :]], axis=1)
            if i == j:
                blk = 0.5 * (blk + blk.T)
            hi, lo = split(blk)
            ghi[256*i:256*i+256, 256*j:256*j+256] = hi
            glo[256*i:256*i+256, 256*j:256*j+256] = lo
            if i != j:
                ghi[256*j:256*j+256, 256*i:256*i+256] = hi.T
                glo[256*j:256*j+256, 256*i:256*i+256] = lo.T
            k += 1
    f_ref[...] = s_ref[...]

    def body(t, _):
        bh, bl = split(f_ref[...])
        b2 = jnp.concatenate([bh, bl], axis=1)
        for i in range(4):
            r2 = dg(ghi[256*i:256*i+256, :], b2, 1, 0)
            r1 = dg(glo[256*i:256*i+256, :], bh, 1, 0)
            img[256*i:256*i+256, :] = r2[:, :128] + (r2[:, 128:] + r1)
        im = img[...]
        a_ref[...] = lax.dot_general(im, im, (((0,), (0,)), ((), ())), precision=HI, preferred_element_type=F32)
        eliminate(a_ref, q_ref, w_ref)
        f_ref[...] = lax.dot_general(img[...], w_ref[...], (((1,), (1,)), ((), ())), precision=HI, preferred_element_type=F32)
        return 0

    lax.fori_loop(0, ITERS, body, 0)
    fh, fl = split(f_ref[...].T)
    f2[:128, :] = fh
    f2[128:, :] = fl
    for c in loads:
        c.wait()
    stores = []
    for n, c in enumerate(pieces):
        h, l = split(u_ref[:, c])
        r = dg(f2[...], h, 1, 0)
        out[:, c] = r[:128, :] + (r[128:, :] + dg(f2[:128, :], l, 1, 0))
        if n % 2 == 1:
            two = slice(c.stop - 1024, c.stop)
            stores.append(pltpu.make_async_copy(out.at[:, two], o_hbm.at[:, two], osem.at[n // 2]))
            stores[-1].start()
    for c in stores:
        c.wait()


def iterate_project(x, s, u):
    v, anyw = pl.BlockSpec(memory_space=pltpu.VMEM), pl.BlockSpec(memory_space=pl.ANY)
    V = pltpu.VMEM
    return pl.pallas_call(
        tail_kernel,
        out_shape=(jax.ShapeDtypeStruct((1024, 128), F32), jax.ShapeDtypeStruct((128, 4096), F32)),
        in_specs=[v, v, anyw], out_specs=(v, anyw),
        scratch_shapes=[V((1024, 1024), BF), V((1024, 1024), BF), V((1024, 128), F32),
                        V((128, 128), F32), V((128, 128), F32), V((128, 128), F32),
                        V((1024, 4096), F32), V((256, 1024), BF), V((128, 4096), F32),
                        pltpu.SemaphoreType.DMA((8,)), pltpu.SemaphoreType.DMA((4,))],
        compiler_params=pltpu.CompilerParams(vmem_limit_bytes=50 << 20),
    )(x, s, u)

MESH = pl.DeviceIdType.MESH
BLOCKS = [(i, j) for j in range(4) for i in range(j + 1)]
STAGES = ((0, 3), (3, 6), (6, 8), (8, 10))
KH = 2048
ORDER = True
LAT = (2.0, 3.9, 3.0)


class Net:
    def __init__(self):
        self.y = lax.axis_index("grp")
        self.inn = lax.axis_index("in")
        self.core = lax.rem(self.inn, 2)
        self.x = lax.rem(self.inn // 2, 4)
        self.z = self.inn // 8

    def axis(self, number):
        a = lax.rem(number, 3)
        ex, ey, ez = (2 - a) * (1 - a) // 2, a * (2 - a), a * (a - 1) // 2
        return Axis(self, ex, ey, ez)

    def twin(self):
        return (self.y, self.inn + 1 - 2 * self.core)

    def barrier(self):
        b = pltpu.get_barrier_semaphore()
        pl.semaphore_signal(b, inc=1, device_id=self.twin(), device_id_type=MESH)
        for e in ((1, 0, 0), (0, 1, 0), (0, 0, 1)):
            for d in (1, 2, 3):
                pl.semaphore_signal(b, inc=1, device_id=Axis(self, *e).peer(d), device_id_type=MESH)
        pl.semaphore_wait(b, 10)


class Axis:
    def __init__(self, net, ex, ey, ez):
        self.net, self.e = net, (ex, ey, ez)
        self.me = net.x * ex + net.y * ey + net.z * ez

    def at(self, d):
        return lax.rem(self.me + d, 4)

    def peer(self, d):
        ex, ey, ez = self.e
        delta = self.at(d) - self.me
        return (self.net.y + delta * ey, self.net.inn + delta * (2 * ex + 8 * ez))


def rows(start, n):
    return pl.ds(pl.multiple_of(start, n), n)


class Reduce:
    def __init__(self, net, x, o, b0, a0, b1, a1, b2, a2, b3, ssem, rsem):
        self.net, self.x, self.o = net, x, o
        self.b0, self.a0, self.b1, self.a1, self.b2, self.a2, self.b3 = b0, a0, b1, a1, b2, a2, b3
        self.ssem, self.rsem = ssem, rsem
        self.flying, self.sent = {}, []
        self.axes = {}
        base = [net.axis(2 * net.core + e) for e in range(3)]
        for s in range(len(STAGES)):
            for p in range(2):
                self.axes[s, p] = [base[(s + p + lvl) % 3] for lvl in range(3)]

    def send(self, src, dst, s, k, dev):
        c = pltpu.make_async_remote_copy(
            src_ref=src, dst_ref=dst, send_sem=self.ssem.at[s, k], recv_sem=self.rsem.at[s, k],
            device_id=dev, device_id_type=MESH,
        )
        c.start()
        self.flying.setdefault(s, []).append(c)

    def land(self, s):
        for c in self.flying.get(s, []):
            c.wait_recv()
        self.sent += self.flying.get(s, [])
        self.flying[s] = []

    def step(self, s, phase):
        u = slice(*STAGES[s])
        core = self.net.core
        self.land(s)
        if phase == 0:
            self.send(self.x.at[u, rows(256 - 256 * core, 256), :], self.b0.at[u], s, 0, self.net.twin())
            return
        if phase == 7:
            half = self.o.at[u, rows(256 * core, 256), :]
            self.send(half, half, s, 31, self.net.twin())
            return
        if phase == 8:
            return
        if phase == 1:
            self.a0[u] = self.x[u, rows(256 * core, 256), :] + self.b0[u]
        for p in range(2):
            x1, x2, x3 = self.axes[s, p]
            if phase == 1:
                for d in (1, 2, 3):
                    src = self.a0.at[u, rows(128 * p + 32 * x1.at(d), 32), :]
                    self.send(src, self.b1.at[p, d - 1, u], s, 1 + 15 * p + d - 1, x1.peer(d))
            if phase == 2:
                own = self.a0[u, rows(128 * p + 32 * x1.me, 32), :]
                self.a1[p, u] = own + (self.b1[p, 0, u] + (self.b1[p, 1, u] + self.b1[p, 2, u]))
                for d in (1, 2, 3):
                    src = self.a1.at[p, u, rows(8 * x2.at(d), 8), :]
                    self.send(src, self.b2.at[p, d - 1, u], s, 4 + 15 * p + d - 1, x2.peer(d))
            if phase == 3:
                own = self.a1[p, u, rows(8 * x2.me, 8), :]
                self.a2[p, u] = own + (self.b2[p, 0, u] + (self.b2[p, 1, u] + self.b2[p, 2, u]))
                for d in (1, 2, 3):
                    self.send(self.a2.at[p, u], self.b3.at[p, d - 1, u], s, 7 + 15 * p + d - 1, x3.peer(d))
            if phase == 4:
                here = self.o.at[u, rows(256 * core + 128 * p + 32 * x1.me + 8 * x2.me, 8), :]
                here[...] = self.ordered(p, u, x3)
                for d in (1, 2, 3):
                    self.send(here, here, s, 10 + 15 * p + d - 1, x2.peer(d))
            if phase == 5:
                here = self.o.at[u, rows(256 * core + 128 * p + 32 * x1.me, 32), :]
                for d in (1, 2, 3):
                    self.send(here, here, s, 13 + 15 * p + d - 1, x1.peer(d))

    def ordered(self, p, u, axis):
        own, t1, t2, t3 = self.a2[p, u], self.b3[p, 0, u], self.b3[p, 1, u], self.b3[p, 2, u]
        even = lax.rem(axis.me, 2) == 0
        near = jnp.where(even, t3, t1)
        far = jnp.where(even, t1, t3)
        return (own + near) + (t2 + far)


PROGRAM = (
    ("wait", 0), ("convert", 0, 0),
    ("wait", 1), ("convert", 0, 1), ("dot", 0, 0), ("dot", 0, 1),
    ("wait", 2), ("convert", 1, 0), ("dot", 1, 0), ("dot", 2, 0), ("convert", 1, 1),
    ("wait", 3), ("dot", 1, 1), ("dot", 2, 1), ("convert", 2, 0), ("check", 3, 7.5),
    ("wait", 4), ("convert", 2, 1), ("dot", 3, 2), ("dot", 4, 2), ("convert", 3, 0), ("check", 5, 11.0),
    ("dot", 5, 2), ("convert", 3, 1), ("check", 6, 12.4),
    ("dot", 6, 2), ("dot", 7, 2), ("check", 8, 15.7),
    ("dot", 8, 2), ("check", 9, 17.4),
    ("dot", 9, 2), ("check", 10, 18.5),
)


def plan():
    ready = {}
    for op in PROGRAM:
        if op[0] == "check":
            for k in range(op[1]):
                ready.setdefault(k, op[2])
    steps = []
    for s, (a, b) in enumerate(STAGES):
        m = b - a
        t = ready[b - 1]
        cost = (LAT[0] + 0.3 * m, LAT[1] + 0.6 * m, LAT[1] + 0.2 * m, LAT[2] + 0.2 * m, LAT[1] + 0.2 * m, LAT[1] + 0.6 * m, 0.0, LAT[0] + 0.3 * m, 0.0)
        for ph in (0, 1, 2, 3, 4, 5, 7, 8):
            steps.append((t, s, ph))
            t += cost[ph]
    return sorted(steps)


def gram_reduce_kernel(u_hbm, o_ref, stg, hl, x, b0, a0, b1, a1, b2, a2, b3, lsem, ssem, rsem, *, comm=True):
    cuts = [(0, 256, 0, 2048), (0, 256, 2048, 4096), (256, 512, 0, 4096), (512, 768, 0, 4096), (768, 1024, 0, 4096)]
    loads = []
    for n, (ra, rb, ca, cb) in enumerate(cuts):
        loads.append(pltpu.make_async_copy(u_hbm.at[ra:rb, ca:cb], stg.at[ra:rb, ca:cb], lsem.at[n]))
        loads[-1].start()
    steps = []
    if comm:
        net = Net()
        net.barrier()
        red = Reduce(net, x, o_ref, b0, a0, b1, a1, b2, a2, b3, ssem, rsem)
        steps = plan()

    def convert(i, h):
        for c in range(KH * h, KH * h + KH, 256):
            hi, lo = split(stg[256 * i:256 * i + 256, c:c + 256])
            hl[i, :256, c:c + 256] = hi
            hl[i, 256:, c:c + 256] = lo

    dst = x if comm else o_ref

    def dot(k, h):
        i, j = BLOCKS[k]
        ks = slice(0, 2 * KH) if h == 2 else slice(KH * h, KH * h + KH)
        if i == j:
            r = dg(hl[i, :256, ks], hl[j, :256, ks], 1, 1) + 2.0 * dg(hl[i, :256, ks], hl[j, 256:, ks], 1, 1)
        else:
            r2 = dg(hl[i, :, ks], hl[j, :256, ks], 1, 1)
            r = r2[:256] + (r2[256:] + dg(hl[i, :256, ks], hl[j, 256:, ks], 1, 1))
        if h == 1:
            dst[k, :256, :] += r[:, :128]
            dst[k, 256:, :] += r[:, 128:]
        else:
            dst[k, :256, :] = r[:, :128]
            dst[k, 256:, :] = r[:, 128:]

    for op in PROGRAM:
        if op[0] == "wait":
            loads[op[1]].wait()
        elif op[0] == "convert":
            convert(*op[1:])
        elif op[0] == "dot":
            dot(*op[1:])
        else:
            while steps and steps[0][0] <= op[2] + 0.01:
                _, s, ph = steps.pop(0)
                red.step(s, ph)
    left = {}
    for _, s, ph in steps:
        left.setdefault(s, []).append(ph)
    while any(left.values()):
        for s in sorted(left, reverse=ORDER):
            if left[s]:
                red.step(s, left[s].pop(0))
    if comm:
        for c in red.sent:
            c.wait_send()


def gram_reduce(u, comm=True):
    v = pl.BlockSpec(memory_space=pltpu.VMEM)
    n = len(STAGES)
    V = pltpu.VMEM
    kw = dict(collective_id=0, has_side_effects=True) if comm else {}
    return pl.pallas_call(
        functools.partial(gram_reduce_kernel, comm=comm),
        out_shape=jax.ShapeDtypeStruct((10, 512, 128), F32),
        in_specs=[pl.BlockSpec(memory_space=pl.ANY)], out_specs=v,
        scratch_shapes=[
            V((1024, 2 * KH), F32), V((4, 512, 2 * KH), BF), V((10, 512, 128), F32),
            V((10, 256, 128), F32), V((10, 256, 128), F32),
            V((2, 3, 10, 32, 128), F32), V((2, 10, 32, 128), F32),
            V((2, 3, 10, 8, 128), F32), V((2, 10, 8, 128), F32), V((2, 3, 10, 8, 128), F32),
            pltpu.SemaphoreType.DMA((5,)), pltpu.SemaphoreType.DMA((n, 32)), pltpu.SemaphoreType.DMA((n, 32)),
        ],
        compiler_params=pltpu.CompilerParams(vmem_limit_bytes=46 << 20, **kw),
    )(u)


def per_device(unfolding, start_basis):
    packed = gram_reduce(unfolding)
    return iterate_project(packed, start_basis, unfolding)


def solution(mesh):
    in_specs = (P(None, ("grp", "in")), P())
    out_specs = (P(), P(None, ("grp", "in")))
    return jax.shard_map(
        per_device, mesh=mesh, in_specs=in_specs, out_specs=out_specs, check_vma=False
    )
```

```python
import functools

import jax
import jax.numpy as jnp
from jax import lax
from jax.experimental import pallas as pl
from jax.experimental.pallas import tpu as pltpu
from jax.sharding import PartitionSpec as P

HI = lax.Precision.HIGHEST
F32 = jnp.float32
BF = jnp.bfloat16

def split(x):
    hi = x.astype(BF)
    return hi, (x - hi.astype(F32)).astype(BF)

def dg(a, b, ca, cb):
    return lax.dot_general(a, b, (((ca,), (cb,)), ((), ())), preferred_element_type=F32)

GROUP = 8


def eliminate(a_ref, q_ref, w_ref):
    sub = lax.broadcasted_iota(jnp.int32, (8, 128), 0)
    lane = lax.broadcasted_iota(jnp.int32, (8, 128), 1)
    wide = lambda v: jnp.broadcast_to(v, (8, 128))
    row = lambda v, r: wide(v[r:r + 1, :])
    col = lambda v, c: wide(v[:, c:c + 1])
    M = [a_ref[8 * p:8 * p + 8, :] for p in range(16)]
    on = [lane == sub + 8 * p for p in range(16)]
    diag = jnp.where(on[0], M[0], 0.0)
    for p in range(1, 16):
        diag = diag + jnp.where(on[p], M[p], 0.0)
    scale = wide(1.0 / jnp.sqrt(jnp.sum(diag, axis=0, keepdims=True)))
    Q = [jnp.where(on[p], scale, 0.0) for p in range(16)]
    for p in range(16):
        M[p] = M[p] * scale * wide(jnp.sum(Q[p], axis=1, keepdims=True))
    done = []
    for p in range(16):
        P, R = M[p], Q[p]
        last = p == 15
        edge = p % GROUP == GROUP - 1
        N, S = (None, None) if edge else (M[p + 1], Q[p + 1])
        cs = [col(P, 8 * p + c) for c in range(8)] if p % GROUP == 0 else gs
        es, gs = [], []
        if not edge:
            es = [col(N, 8 * p + c) for c in range(8)]
            gs = [col(N, 8 * p + 8 + c) for c in range(8)]
        dv = rv = tv = jnp.zeros((8, 128), F32)
        for r in range(0, 8, 2):
            a, b, d = row(cs[r], r), row(cs[r], r + 1), row(cs[r + 1], r + 1)
            det = a * d - b * b
            rdet = 1.0 / det
            ra = 1.0 / a
            dv = jnp.where(sub == r, a, jnp.where(sub == r + 1, det * ra, dv))
            rv = jnp.where(sub == r, ra, jnp.where(sub == r + 1, a * rdet, rv))
            tv = jnp.where(sub == r + 1, b * ra, tv)
            sets = []
            if r < 6:
                below = sub > r + 1
                sets.append((jnp.where(below, d * cs[r] - b * cs[r + 1], 0.0),
                             jnp.where(below, a * cs[r + 1] - b * cs[r], 0.0)))
            if not edge:
                sets.append((d * es[r] - b * es[r + 1], a * es[r + 1] - b * es[r]))
            p0, p1, q0, q1 = row(P, r), row(P, r + 1), row(R, r), row(R, r + 1)
            for k in range(r + 2, 8):
                s0, s1 = row(cs[k], r), row(cs[k], r + 1)
                if not edge:
                    n0, n1 = sets[-1]
                    es[k] = es[k] - rdet * (n0 * s0 + n1 * s1)
                n0, n1 = sets[0]
                cs[k] = cs[k] - rdet * (n0 * s0 + n1 * s1)
            for k in range(8 if not edge else 0):
                s0, s1 = row(es[r], k), row(es[r + 1], k)
                n0, n1 = sets[-1]
                gs[k] = gs[k] - rdet * (n0 * s0 + n1 * s1)
            if r < 6:
                n0, n1 = sets[0]
                P = P - rdet * (n0 * p0 + n1 * p1)
                R = R - rdet * (n0 * q0 + n1 * q1)
            if not edge:
                n0, n1 = sets[-1]
                N = N - rdet * (n0 * p0 + n1 * p1)
                S = S - rdet * (n0 * q0 + n1 * q1)
        P = P - tv * pltpu.roll(P, 1, 0)
        R = R - tv * pltpu.roll(R, 1, 0)
        w_ref[8 * p:8 * p + 8, :] = R * (1.0 / jnp.sqrt(dv))
        if not edge:
            M[p + 1], Q[p + 1] = N, S
        done.append((P, R, P * rv))
        group = p // GROUP
        stop = GROUP * group + GROUP
        if p + 2 < min(stop, 16):
            T = jnp.transpose(P * rv)
            pr = [row(P, r) for r in range(8)]
            qr = [row(R, r) for r in range(8)]
            for i in range(p + 2, stop):
                for r in range(8):
                    mm = wide(T[8 * i:8 * i + 8, r:r + 1])
                    M[i] = M[i] - mm * pr[r]
                    Q[i] = Q[i] - mm * qr[r]
        if p == stop - 1 and not last:
            parts = done[GROUP * group:]
            left = jnp.concatenate([v[2] for v in parts], axis=0)
            right = jnp.concatenate([jnp.concatenate(v[:2], axis=1) for v in parts], axis=0)
            upd = lax.dot_general(left, right, (((0,), (0,)), ((), ())), precision=HI, preferred_element_type=F32)
            for i in range(stop, 16):
                M[i] = M[i] - upd[8 * i:8 * i + 8, :128]
                Q[i] = Q[i] - upd[8 * i:8 * i + 8, 128:]


ITERS = 3


def tail_kernel(x_ref, s_ref, u_hbm, f_ref, o_hbm, ghi, glo, img, a_ref, q_ref, w_ref, u_ref, f2, out, lsem, osem):
    pieces = [slice(c, c + 512) for c in range(0, 4096, 512)]
    loads = [pltpu.make_async_copy(u_hbm.at[:, c], u_ref.at[:, c], lsem.at[n]) for n, c in enumerate(pieces)]
    for c in loads:
        c.start()
    k = 0
    for j in range(4):
        for i in range(j + 1):
            blk = jnp.concatenate([x_ref[k, :256, :], x_ref[k, 256:, :]], axis=1)
            if i == j:
                blk = 0.5 * (blk + blk.T)
            hi, lo = split(blk)
            ghi[256*i:256*i+256, 256*j:256*j+256] = hi
            glo[256*i:256*i+256, 256*j:256*j+256] = lo
            if i != j:
                ghi[256*j:256*j+256, 256*i:256*i+256] = hi.T
                glo[256*j:256*j+256, 256*i:256*i+256] = lo.T
            k += 1
    f_ref[...] = s_ref[...]

    def body(t, _):
        bh, bl = split(f_ref[...])
        b2 = jnp.concatenate([bh, bl], axis=1)
        for i in range(4):
            r2 = dg(ghi[256*i:256*i+256, :], b2, 1, 0)
            r1 = dg(glo[256*i:256*i+256, :], bh, 1, 0)
            img[256*i:256*i+256, :] = r2[:, :128] + (r2[:, 128:] + r1)
        im = img[...]
        a_ref[...] = lax.dot_general(im, im, (((0,), (0,)), ((), ())), precision=HI, preferred_element_type=F32)
        eliminate(a_ref, q_ref, w_ref)
        f_ref[...] = lax.dot_general(img[...], w_ref[...], (((1,), (1,)), ((), ())), precision=HI, preferred_element_type=F32)
        return 0

    lax.fori_loop(0, ITERS, body, 0)
    fh, fl = split(f_ref[...].T)
    f2[:128, :] = fh
    f2[128:, :] = fl
    for c in loads:
        c.wait()
    stores = []
    for n, c in enumerate(pieces):
        h, l = split(u_ref[:, c])
        r = dg(f2[...], h, 1, 0)
        out[:, c] = r[:128, :] + (r[128:, :] + dg(f2[:128, :], l, 1, 0))
        if n % 2 == 1:
            two = slice(c.stop - 1024, c.stop)
            stores.append(pltpu.make_async_copy(out.at[:, two], o_hbm.at[:, two], osem.at[n // 2]))
            stores[-1].start()
    for c in stores:
        c.wait()


def iterate_project(x, s, u):
    v, anyw = pl.BlockSpec(memory_space=pltpu.VMEM), pl.BlockSpec(memory_space=pl.ANY)
    V = pltpu.VMEM
    return pl.pallas_call(
        tail_kernel,
        out_shape=(jax.ShapeDtypeStruct((1024, 128), F32), jax.ShapeDtypeStruct((128, 4096), F32)),
        in_specs=[v, v, anyw], out_specs=(v, anyw),
        scratch_shapes=[V((1024, 1024), BF), V((1024, 1024), BF), V((1024, 128), F32),
                        V((128, 128), F32), V((128, 128), F32), V((128, 128), F32),
                        V((1024, 4096), F32), V((256, 1024), BF), V((128, 4096), F32),
                        pltpu.SemaphoreType.DMA((8,)), pltpu.SemaphoreType.DMA((4,))],
        compiler_params=pltpu.CompilerParams(vmem_limit_bytes=50 << 20),
    )(x, s, u)

MESH = pl.DeviceIdType.MESH
BLOCKS = [(i, j) for j in range(4) for i in range(j + 1)]
STAGES = ((0, 3), (3, 6), (6, 8), (8, 10))
KH = 2048
ORDER = True
LAT = (2.0, 3.9, 3.0)


class Net:
    def __init__(self):
        self.y = lax.axis_index("grp")
        self.inn = lax.axis_index("in")
        self.core = lax.rem(self.inn, 2)
        self.x = lax.rem(self.inn // 2, 4)
        self.z = self.inn // 8

    def axis(self, number):
        a = lax.rem(number, 3)
        ex, ey, ez = (2 - a) * (1 - a) // 2, a * (2 - a), a * (a - 1) // 2
        return Axis(self, ex, ey, ez)

    def twin(self):
        return (self.y, self.inn + 1 - 2 * self.core)

    def greet(self):
        b = pltpu.get_barrier_semaphore()
        pl.semaphore_signal(b, inc=1, device_id=self.twin(), device_id_type=MESH)
        for e in ((1, 0, 0), (0, 1, 0), (0, 0, 1)):
            for d in (1, 2, 3):
                pl.semaphore_signal(b, inc=1, device_id=Axis(self, *e).peer(d), device_id_type=MESH)

    def meet(self):
        pl.semaphore_wait(pltpu.get_barrier_semaphore(), 10)


class Axis:
    def __init__(self, net, ex, ey, ez):
        self.net, self.e = net, (ex, ey, ez)
        self.me = net.x * ex + net.y * ey + net.z * ez

    def at(self, d):
        return lax.rem(self.me + d, 4)

    def peer(self, d):
        ex, ey, ez = self.e
        delta = self.at(d) - self.me
        return (self.net.y + delta * ey, self.net.inn + delta * (2 * ex + 8 * ez))


def rows(start, n):
    return pl.ds(pl.multiple_of(start, n), n)


class Reduce:
    def __init__(self, net, x, o, b0, a0, b1, a1, b2, a2, b3, ssem, rsem):
        self.net, self.x, self.o = net, x, o
        self.b0, self.a0, self.b1, self.a1, self.b2, self.a2, self.b3 = b0, a0, b1, a1, b2, a2, b3
        self.ssem, self.rsem = ssem, rsem
        self.flying, self.sent = {}, []
        self.axes = {}
        base = [net.axis(2 * net.core + e) for e in range(3)]
        for s in range(len(STAGES)):
            for p in range(2):
                self.axes[s, p] = [base[(s + p + lvl) % 3] for lvl in range(3)]

    def send(self, src, dst, s, k, dev):
        c = pltpu.make_async_remote_copy(
            src_ref=src, dst_ref=dst, send_sem=self.ssem.at[s, k], recv_sem=self.rsem.at[s, k],
            device_id=dev, device_id_type=MESH,
        )
        c.start()
        self.flying.setdefault(s, []).append(c)

    def land(self, s):
        for c in self.flying.get(s, []):
            c.wait_recv()
        self.sent += self.flying.get(s, [])
        self.flying[s] = []

    def step(self, s, phase):
        u = slice(*STAGES[s])
        core = self.net.core
        self.land(s)
        if phase == 0:
            self.send(self.x.at[u, rows(256 - 256 * core, 256), :], self.b0.at[u], s, 0, self.net.twin())
            return
        if phase == 7:
            half = self.o.at[u, rows(256 * core, 256), :]
            self.send(half, half, s, 31, self.net.twin())
            return
        if phase == 8:
            return
        if phase == 1:
            self.a0[u] = self.x[u, rows(256 * core, 256), :] + self.b0[u]
        for p in range(2):
            x1, x2, x3 = self.axes[s, p]
            if phase == 1:
                for d in (1, 2, 3):
                    src = self.a0.at[u, rows(128 * p + 32 * x1.at(d), 32), :]
                    self.send(src, self.b1.at[p, d - 1, u], s, 1 + 15 * p + d - 1, x1.peer(d))
            if phase == 2:
                own = self.a0[u, rows(128 * p + 32 * x1.me, 32), :]
                self.a1[p, u] = own + (self.b1[p, 0, u] + (self.b1[p, 1, u] + self.b1[p, 2, u]))
                for d in (1, 2, 3):
                    src = self.a1.at[p, u, rows(8 * x2.at(d), 8), :]
                    self.send(src, self.b2.at[p, d - 1, u], s, 4 + 15 * p + d - 1, x2.peer(d))
            if phase == 3:
                own = self.a1[p, u, rows(8 * x2.me, 8), :]
                self.a2[p, u] = own + (self.b2[p, 0, u] + (self.b2[p, 1, u] + self.b2[p, 2, u]))
                for d in (1, 2, 3):
                    self.send(self.a2.at[p, u], self.b3.at[p, d - 1, u], s, 7 + 15 * p + d - 1, x3.peer(d))
            if phase == 4:
                here = self.o.at[u, rows(256 * core + 128 * p + 32 * x1.me + 8 * x2.me, 8), :]
                here[...] = self.ordered(p, u, x3)
                for d in (1, 2, 3):
                    self.send(here, here, s, 10 + 15 * p + d - 1, x2.peer(d))
            if phase == 5:
                here = self.o.at[u, rows(256 * core + 128 * p + 32 * x1.me, 32), :]
                for d in (1, 2, 3):
                    self.send(here, here, s, 13 + 15 * p + d - 1, x1.peer(d))

    def ordered(self, p, u, axis):
        own, t1, t2, t3 = self.a2[p, u], self.b3[p, 0, u], self.b3[p, 1, u], self.b3[p, 2, u]
        even = lax.rem(axis.me, 2) == 0
        near = jnp.where(even, t3, t1)
        far = jnp.where(even, t1, t3)
        return (own + near) + (t2 + far)


PROGRAM = (
    ("wait", 0), ("convert", 0, 0),
    ("wait", 1), ("convert", 0, 1), ("dot", 0, 0), ("dot", 0, 1),
    ("wait", 2), ("convert", 1, 0), ("dot", 1, 0), ("dot", 2, 0), ("convert", 1, 1),
    ("wait", 3), ("dot", 1, 1), ("dot", 2, 1), ("convert", 2, 0), ("check", 3, 7.5),
    ("wait", 4), ("convert", 2, 1), ("dot", 3, 2), ("dot", 4, 2), ("convert", 3, 0), ("check", 5, 11.0),
    ("dot", 5, 2), ("convert", 3, 1), ("check", 6, 12.4),
    ("dot", 6, 2), ("dot", 7, 2), ("check", 8, 15.7),
    ("dot", 8, 2), ("check", 9, 17.4),
    ("dot", 9, 2), ("check", 10, 18.5),
)


def plan():
    ready = {}
    for op in PROGRAM:
        if op[0] == "check":
            for k in range(op[1]):
                ready.setdefault(k, op[2])
    steps = []
    for s, (a, b) in enumerate(STAGES):
        m = b - a
        t = ready[b - 1]
        cost = (LAT[0] + 0.3 * m, LAT[1] + 0.6 * m, LAT[1] + 0.2 * m, LAT[2] + 0.2 * m, LAT[1] + 0.2 * m, LAT[1] + 0.6 * m, 0.0, LAT[0] + 0.3 * m, 0.0)
        for ph in (0, 1, 2, 3, 4, 5, 7, 8):
            steps.append((t, s, ph))
            t += cost[ph]
    return sorted(steps)


def gram_reduce_kernel(u_hbm, o_ref, stg, hl, x, b0, a0, b1, a1, b2, a2, b3, lsem, ssem, rsem, *, comm=True):
    cuts = [(0, 256, 0, 2048), (0, 256, 2048, 4096), (256, 512, 0, 4096), (512, 768, 0, 4096), (768, 1024, 0, 4096)]
    loads = []
    for n, (ra, rb, ca, cb) in enumerate(cuts):
        loads.append(pltpu.make_async_copy(u_hbm.at[ra:rb, ca:cb], stg.at[ra:rb, ca:cb], lsem.at[n]))
        loads[-1].start()
    steps = []
    if comm:
        net = Net()
        net.greet()
        red = Reduce(net, x, o_ref, b0, a0, b1, a1, b2, a2, b3, ssem, rsem)
        steps = plan()

    def convert(i, h):
        for c in range(KH * h, KH * h + KH, 256):
            hi, lo = split(stg[256 * i:256 * i + 256, c:c + 256])
            hl[i, :256, c:c + 256] = hi
            hl[i, 256:, c:c + 256] = lo

    dst = x if comm else o_ref

    def dot(k, h):
        i, j = BLOCKS[k]
        ks = slice(0, 2 * KH) if h == 2 else slice(KH * h, KH * h + KH)
        if i == j:
            r = dg(hl[i, :256, ks], hl[j, :256, ks], 1, 1) + 2.0 * dg(hl[i, :256, ks], hl[j, 256:, ks], 1, 1)
        else:
            r2 = dg(hl[i, :, ks], hl[j, :256, ks], 1, 1)
            r = r2[:256] + (r2[256:] + dg(hl[i, :256, ks], hl[j, 256:, ks], 1, 1))
        if h == 1:
            dst[k, :256, :] += r[:, :128]
            dst[k, 256:, :] += r[:, 128:]
        else:
            dst[k, :256, :] = r[:, :128]
            dst[k, 256:, :] = r[:, 128:]

    for op in PROGRAM:
        if op[0] == "wait":
            loads[op[1]].wait()
        elif op[0] == "convert":
            convert(*op[1:])
        elif op[0] == "dot":
            dot(*op[1:])
        else:
            if comm and op[1] == 3:
                net.meet()
            while steps and steps[0][0] <= op[2] + 0.01:
                _, s, ph = steps.pop(0)
                red.step(s, ph)
    left = {}
    for _, s, ph in steps:
        left.setdefault(s, []).append(ph)
    while any(left.values()):
        for s in sorted(left, reverse=ORDER):
            if left[s]:
                red.step(s, left[s].pop(0))
    if comm:
        for c in red.sent:
            c.wait_send()


def gram_reduce(u, comm=True):
    v = pl.BlockSpec(memory_space=pltpu.VMEM)
    n = len(STAGES)
    V = pltpu.VMEM
    kw = dict(collective_id=0, has_side_effects=True) if comm else {}
    return pl.pallas_call(
        functools.partial(gram_reduce_kernel, comm=comm),
        out_shape=jax.ShapeDtypeStruct((10, 512, 128), F32),
        in_specs=[pl.BlockSpec(memory_space=pl.ANY)], out_specs=v,
        scratch_shapes=[
            V((1024, 2 * KH), F32), V((4, 512, 2 * KH), BF), V((10, 512, 128), F32),
            V((10, 256, 128), F32), V((10, 256, 128), F32),
            V((2, 3, 10, 32, 128), F32), V((2, 10, 32, 128), F32),
            V((2, 3, 10, 8, 128), F32), V((2, 10, 8, 128), F32), V((2, 3, 10, 8, 128), F32),
            pltpu.SemaphoreType.DMA((5,)), pltpu.SemaphoreType.DMA((n, 32)), pltpu.SemaphoreType.DMA((n, 32)),
        ],
        compiler_params=pltpu.CompilerParams(vmem_limit_bytes=46 << 20, **kw),
    )(u)


def per_device(unfolding, start_basis):
    packed = gram_reduce(unfolding)
    return iterate_project(packed, start_basis, unfolding)


def solution(mesh):
    in_specs = (P(None, ("grp", "in")), P())
    out_specs = (P(), P(None, ("grp", "in")))
    return jax.shard_map(
        per_device, mesh=mesh, in_specs=in_specs, out_specs=out_specs, check_vma=False
    )
```

```python
import functools

import jax
import jax.numpy as jnp
from jax import lax
from jax.experimental import pallas as pl
from jax.experimental.pallas import tpu as pltpu
from jax.sharding import PartitionSpec as P

HI = lax.Precision.HIGHEST
F32 = jnp.float32
BF = jnp.bfloat16

def split(x):
    hi = x.astype(BF)
    return hi, (x - hi.astype(F32)).astype(BF)

def dg(a, b, ca, cb):
    return lax.dot_general(a, b, (((ca,), (cb,)), ((), ())), preferred_element_type=F32)

GROUP = 8


def eliminate(a_ref, q_ref, w_ref):
    sub = lax.broadcasted_iota(jnp.int32, (8, 128), 0)
    lane = lax.broadcasted_iota(jnp.int32, (8, 128), 1)
    wide = lambda v: jnp.broadcast_to(v, (8, 128))
    row = lambda v, r: wide(v[r:r + 1, :])
    col = lambda v, c: wide(v[:, c:c + 1])
    M = [a_ref[8 * p:8 * p + 8, :] for p in range(16)]
    on = [lane == sub + 8 * p for p in range(16)]
    diag = jnp.where(on[0], M[0], 0.0)
    for p in range(1, 16):
        diag = diag + jnp.where(on[p], M[p], 0.0)
    scale = wide(1.0 / jnp.sqrt(jnp.sum(diag, axis=0, keepdims=True)))
    Q = [jnp.where(on[p], scale, 0.0) for p in range(16)]
    for p in range(16):
        M[p] = M[p] * scale * wide(jnp.sum(Q[p], axis=1, keepdims=True))
    done = []
    for p in range(16):
        P, R = M[p], Q[p]
        last = p == 15
        edge = p % GROUP == GROUP - 1
        N, S = (None, None) if edge else (M[p + 1], Q[p + 1])
        cs = [col(P, 8 * p + c) for c in range(8)] if p % GROUP == 0 else gs
        es, gs = [], []
        if not edge:
            es = [col(N, 8 * p + c) for c in range(8)]
            gs = [col(N, 8 * p + 8 + c) for c in range(8)]
        dv = rv = tv = jnp.zeros((8, 128), F32)
        for r in range(0, 8, 2):
            a, b, d = row(cs[r], r), row(cs[r], r + 1), row(cs[r + 1], r + 1)
            det = a * d - b * b
            rdet = 1.0 / det
            ra = 1.0 / a
            dv = jnp.where(sub == r, a, jnp.where(sub == r + 1, det * ra, dv))
            rv = jnp.where(sub == r, ra, jnp.where(sub == r + 1, a * rdet, rv))
            tv = jnp.where(sub == r + 1, b * ra, tv)
            sets = []
            if r < 6:
                below = sub > r + 1
                sets.append((jnp.where(below, d * cs[r] - b * cs[r + 1], 0.0),
                             jnp.where(below, a * cs[r + 1] - b * cs[r], 0.0)))
            if not edge:
                sets.append((d * es[r] - b * es[r + 1], a * es[r + 1] - b * es[r]))
            p0, p1, q0, q1 = row(P, r), row(P, r + 1), row(R, r), row(R, r + 1)
            for k in range(r + 2, 8):
                s0, s1 = row(cs[k], r), row(cs[k], r + 1)
                if not edge:
                    n0, n1 = sets[-1]
                    es[k] = es[k] - rdet * (n0 * s0 + n1 * s1)
                n0, n1 = sets[0]
                cs[k] = cs[k] - rdet * (n0 * s0 + n1 * s1)
            for k in range(8 if not edge else 0):
                s0, s1 = row(es[r], k), row(es[r + 1], k)
                n0, n1 = sets[-1]
                gs[k] = gs[k] - rdet * (n0 * s0 + n1 * s1)
            if r < 6:
                n0, n1 = sets[0]
                P = P - rdet * (n0 * p0 + n1 * p1)
                R = R - rdet * (n0 * q0 + n1 * q1)
            if not edge:
                n0, n1 = sets[-1]
                N = N - rdet * (n0 * p0 + n1 * p1)
                S = S - rdet * (n0 * q0 + n1 * q1)
        P = P - tv * pltpu.roll(P, 1, 0)
        R = R - tv * pltpu.roll(R, 1, 0)
        w_ref[8 * p:8 * p + 8, :] = R * (1.0 / jnp.sqrt(dv))
        if not edge:
            M[p + 1], Q[p + 1] = N, S
        done.append((P, R, P * rv))
        group = p // GROUP
        stop = GROUP * group + GROUP
        if p + 2 < min(stop, 16):
            T = jnp.transpose(P * rv)
            pr = [row(P, r) for r in range(8)]
            qr = [row(R, r) for r in range(8)]
            for i in range(p + 2, stop):
                for r in range(8):
                    mm = wide(T[8 * i:8 * i + 8, r:r + 1])
                    M[i] = M[i] - mm * pr[r]
                    Q[i] = Q[i] - mm * qr[r]
        if p == stop - 1 and not last:
            parts = done[GROUP * group:]
            left = jnp.concatenate([v[2] for v in parts], axis=0)
            right = jnp.concatenate([jnp.concatenate(v[:2], axis=1) for v in parts], axis=0)
            upd = lax.dot_general(left, right, (((0,), (0,)), ((), ())), precision=HI, preferred_element_type=F32)
            for i in range(stop, 16):
                M[i] = M[i] - upd[8 * i:8 * i + 8, :128]
                Q[i] = Q[i] - upd[8 * i:8 * i + 8, 128:]


ITERS = 3


def tail_kernel(x_ref, s_ref, u_hbm, f_ref, o_hbm, ghi, glo, img, a_ref, q_ref, w_ref, u_ref, f2, out, lsem, osem):
    pieces = [slice(c, c + 512) for c in range(0, 4096, 512)]
    loads = [pltpu.make_async_copy(u_hbm.at[:, c], u_ref.at[:, c], lsem.at[n]) for n, c in enumerate(pieces)]
    for c in loads:
        c.start()
    k = 0
    for j in range(4):
        for i in range(j + 1):
            blk = jnp.concatenate([x_ref[k, :256, :], x_ref[k, 256:, :]], axis=1)
            if i == j:
                blk = 0.5 * (blk + blk.T)
            hi, lo = split(blk)
            ghi[256*i:256*i+256, 256*j:256*j+256] = hi
            glo[256*i:256*i+256, 256*j:256*j+256] = lo
            if i != j:
                ghi[256*j:256*j+256, 256*i:256*i+256] = hi.T
                glo[256*j:256*j+256, 256*i:256*i+256] = lo.T
            k += 1
    f_ref[...] = s_ref[...]

    def body(t, _):
        bh, bl = split(f_ref[...])
        b2 = jnp.concatenate([bh, bl], axis=1)
        for i in range(4):
            r2 = dg(ghi[256*i:256*i+256, :], b2, 1, 0)
            r1 = dg(glo[256*i:256*i+256, :], bh, 1, 0)
            img[256*i:256*i+256, :] = r2[:, :128] + (r2[:, 128:] + r1)
        im = img[...]
        a_ref[...] = lax.dot_general(im, im, (((0,), (0,)), ((), ())), precision=HI, preferred_element_type=F32)
        eliminate(a_ref, q_ref, w_ref)
        ih, il = split(img[...])
        wh, wl = split(w_ref[...])
        r2 = dg(ih, jnp.concatenate([wh, wl], axis=0), 1, 1)
        f_ref[...] = r2[:, :128] + (r2[:, 128:] + dg(il, wh, 1, 1))
        return 0

    lax.fori_loop(0, ITERS, body, 0)
    fh, fl = split(f_ref[...].T)
    f2[:128, :] = fh
    f2[128:, :] = fl
    for c in loads:
        c.wait()
    stores = []
    for n, c in enumerate(pieces):
        h, l = split(u_ref[:, c])
        r = dg(f2[...], h, 1, 0)
        out[:, c] = r[:128, :] + (r[128:, :] + dg(f2[:128, :], l, 1, 0))
        if n % 2 == 1:
            two = slice(c.stop - 1024, c.stop)
            stores.append(pltpu.make_async_copy(out.at[:, two], o_hbm.at[:, two], osem.at[n // 2]))
            stores[-1].start()
    for c in stores:
        c.wait()


def iterate_project(x, s, u):
    v, anyw = pl.BlockSpec(memory_space=pltpu.VMEM), pl.BlockSpec(memory_space=pl.ANY)
    V = pltpu.VMEM
    return pl.pallas_call(
        tail_kernel,
        out_shape=(jax.ShapeDtypeStruct((1024, 128), F32), jax.ShapeDtypeStruct((128, 4096), F32)),
        in_specs=[v, v, anyw], out_specs=(v, anyw),
        scratch_shapes=[V((1024, 1024), BF), V((1024, 1024), BF), V((1024, 128), F32),
                        V((128, 128), F32), V((128, 128), F32), V((128, 128), F32),
                        V((1024, 4096), F32), V((256, 1024), BF), V((128, 4096), F32),
                        pltpu.SemaphoreType.DMA((8,)), pltpu.SemaphoreType.DMA((4,))],
        compiler_params=pltpu.CompilerParams(vmem_limit_bytes=50 << 20),
    )(x, s, u)

MESH = pl.DeviceIdType.MESH
BLOCKS = [(i, j) for j in range(4) for i in range(j + 1)]
STAGES = ((0, 3), (3, 6), (6, 8), (8, 10))
KH = 2048
ORDER = True
LAT = (2.0, 3.9, 3.0)


class Net:
    def __init__(self):
        self.y = lax.axis_index("grp")
        self.inn = lax.axis_index("in")
        self.core = lax.rem(self.inn, 2)
        self.x = lax.rem(self.inn // 2, 4)
        self.z = self.inn // 8

    def axis(self, number):
        a = lax.rem(number, 3)
        ex, ey, ez = (2 - a) * (1 - a) // 2, a * (2 - a), a * (a - 1) // 2
        return Axis(self, ex, ey, ez)

    def twin(self):
        return (self.y, self.inn + 1 - 2 * self.core)

    def greet(self):
        b = pltpu.get_barrier_semaphore()
        pl.semaphore_signal(b, inc=1, device_id=self.twin(), device_id_type=MESH)
        for e in ((1, 0, 0), (0, 1, 0), (0, 0, 1)):
            for d in (1, 2, 3):
                pl.semaphore_signal(b, inc=1, device_id=Axis(self, *e).peer(d), device_id_type=MESH)

    def meet(self):
        pl.semaphore_wait(pltpu.get_barrier_semaphore(), 10)


class Axis:
    def __init__(self, net, ex, ey, ez):
        self.net, self.e = net, (ex, ey, ez)
        self.me = net.x * ex + net.y * ey + net.z * ez

    def at(self, d):
        return lax.rem(self.me + d, 4)

    def peer(self, d):
        ex, ey, ez = self.e
        delta = self.at(d) - self.me
        return (self.net.y + delta * ey, self.net.inn + delta * (2 * ex + 8 * ez))


def rows(start, n):
    return pl.ds(pl.multiple_of(start, n), n)


class Reduce:
    def __init__(self, net, x, o, b0, a0, b1, a1, b2, a2, b3, ssem, rsem):
        self.net, self.x, self.o = net, x, o
        self.b0, self.a0, self.b1, self.a1, self.b2, self.a2, self.b3 = b0, a0, b1, a1, b2, a2, b3
        self.ssem, self.rsem = ssem, rsem
        self.flying, self.sent = {}, []
        self.axes = {}
        base = [net.axis(2 * net.core + e) for e in range(3)]
        for s in range(len(STAGES)):
            for p in range(2):
                self.axes[s, p] = [base[(s + p + lvl) % 3] for lvl in range(3)]

    def send(self, src, dst, s, k, dev):
        c = pltpu.make_async_remote_copy(
            src_ref=src, dst_ref=dst, send_sem=self.ssem.at[s, k], recv_sem=self.rsem.at[s, k],
            device_id=dev, device_id_type=MESH,
        )
        c.start()
        self.flying.setdefault(s, []).append(c)

    def land(self, s):
        for c in self.flying.get(s, []):
            c.wait_recv()
        self.sent += self.flying.get(s, [])
        self.flying[s] = []

    def step(self, s, phase):
        u = slice(*STAGES[s])
        core = self.net.core
        self.land(s)
        if phase == 0:
            self.send(self.x.at[u, rows(256 - 256 * core, 256), :], self.b0.at[u], s, 0, self.net.twin())
            return
        if phase == 7:
            half = self.o.at[u, rows(256 * core, 256), :]
            self.send(half, half, s, 31, self.net.twin())
            return
        if phase == 8:
            return
        if phase == 1:
            self.a0[u] = self.x[u, rows(256 * core, 256), :] + self.b0[u]
        for p in range(2):
            x1, x2, x3 = self.axes[s, p]
            if phase == 1:
                for d in (1, 2, 3):
                    src = self.a0.at[u, rows(128 * p + 32 * x1.at(d), 32), :]
                    self.send(src, self.b1.at[p, d - 1, u], s, 1 + 15 * p + d - 1, x1.peer(d))
            if phase == 2:
                own = self.a0[u, rows(128 * p + 32 * x1.me, 32), :]
                self.a1[p, u] = own + (self.b1[p, 0, u] + (self.b1[p, 1, u] + self.b1[p, 2, u]))
                for d in (1, 2, 3):
                    src = self.a1.at[p, u, rows(8 * x2.at(d), 8), :]
                    self.send(src, self.b2.at[p, d - 1, u], s, 4 + 15 * p + d - 1, x2.peer(d))
            if phase == 3:
                own = self.a1[p, u, rows(8 * x2.me, 8), :]
                self.a2[p, u] = own + (self.b2[p, 0, u] + (self.b2[p, 1, u] + self.b2[p, 2, u]))
                for d in (1, 2, 3):
                    self.send(self.a2.at[p, u], self.b3.at[p, d - 1, u], s, 7 + 15 * p + d - 1, x3.peer(d))
            if phase == 4:
                here = self.o.at[u, rows(256 * core + 128 * p + 32 * x1.me + 8 * x2.me, 8), :]
                here[...] = self.ordered(p, u, x3)
                for d in (1, 2, 3):
                    self.send(here, here, s, 10 + 15 * p + d - 1, x2.peer(d))
            if phase == 5:
                here = self.o.at[u, rows(256 * core + 128 * p + 32 * x1.me, 32), :]
                for d in (1, 2, 3):
                    self.send(here, here, s, 13 + 15 * p + d - 1, x1.peer(d))

    def ordered(self, p, u, axis):
        own, t1, t2, t3 = self.a2[p, u], self.b3[p, 0, u], self.b3[p, 1, u], self.b3[p, 2, u]
        even = lax.rem(axis.me, 2) == 0
        near = jnp.where(even, t3, t1)
        far = jnp.where(even, t1, t3)
        return (own + near) + (t2 + far)


PROGRAM = (
    ("wait", 0), ("convert", 0, 0),
    ("wait", 1), ("convert", 0, 1), ("dot", 0, 0), ("dot", 0, 1),
    ("wait", 2), ("convert", 1, 0), ("dot", 1, 0), ("dot", 2, 0), ("convert", 1, 1),
    ("wait", 3), ("dot", 1, 1), ("dot", 2, 1), ("convert", 2, 0), ("check", 3, 7.5),
    ("wait", 4), ("convert", 2, 1), ("dot", 3, 2), ("dot", 4, 2), ("convert", 3, 0), ("check", 5, 11.0),
    ("dot", 5, 2), ("convert", 3, 1), ("check", 6, 12.4),
    ("dot", 6, 2), ("dot", 7, 2), ("check", 8, 15.7),
    ("dot", 8, 2), ("check", 9, 17.4),
    ("dot", 9, 2), ("check", 10, 18.5),
)


def plan():
    ready = {}
    for op in PROGRAM:
        if op[0] == "check":
            for k in range(op[1]):
                ready.setdefault(k, op[2])
    steps = []
    for s, (a, b) in enumerate(STAGES):
        m = b - a
        t = ready[b - 1]
        cost = (LAT[0] + 0.3 * m, LAT[1] + 0.6 * m, LAT[1] + 0.2 * m, LAT[2] + 0.2 * m, LAT[1] + 0.2 * m, LAT[1] + 0.6 * m, 0.0, LAT[0] + 0.3 * m, 0.0)
        for ph in (0, 1, 2, 3, 4, 5, 7, 8):
            steps.append((t, s, ph))
            t += cost[ph]
    return sorted(steps)


def gram_reduce_kernel(u_hbm, o_ref, stg, hl, x, b0, a0, b1, a1, b2, a2, b3, lsem, ssem, rsem, *, comm=True):
    cuts = [(0, 256, 0, 2048), (0, 256, 2048, 4096), (256, 512, 0, 4096), (512, 768, 0, 4096), (768, 1024, 0, 4096)]
    loads = []
    for n, (ra, rb, ca, cb) in enumerate(cuts):
        loads.append(pltpu.make_async_copy(u_hbm.at[ra:rb, ca:cb], stg.at[ra:rb, ca:cb], lsem.at[n]))
        loads[-1].start()
    steps = []
    if comm:
        net = Net()
        net.greet()
        red = Reduce(net, x, o_ref, b0, a0, b1, a1, b2, a2, b3, ssem, rsem)
        steps = plan()

    def convert(i, h):
        for c in range(KH * h, KH * h + KH, 256):
            hi, lo = split(stg[256 * i:256 * i + 256, c:c + 256])
            hl[i, :256, c:c + 256] = hi
            hl[i, 256:, c:c + 256] = lo

    dst = x if comm else o_ref

    def dot(k, h):
        i, j = BLOCKS[k]
        ks = slice(0, 2 * KH) if h == 2 else slice(KH * h, KH * h + KH)
        if i == j:
            r = dg(hl[i, :256, ks], hl[j, :256, ks], 1, 1) + 2.0 * dg(hl[i, :256, ks], hl[j, 256:, ks], 1, 1)
        else:
            r2 = dg(hl[i, :, ks], hl[j, :256, ks], 1, 1)
            r = r2[:256] + (r2[256:] + dg(hl[i, :256, ks], hl[j, 256:, ks], 1, 1))
        if h == 1:
            dst[k, :256, :] += r[:, :128]
            dst[k, 256:, :] += r[:, 128:]
        else:
            dst[k, :256, :] = r[:, :128]
            dst[k, 256:, :] = r[:, 128:]

    for op in PROGRAM:
        if op[0] == "wait":
            loads[op[1]].wait()
        elif op[0] == "convert":
            convert(*op[1:])
        elif op[0] == "dot":
            dot(*op[1:])
        else:
            if comm and op[1] == 3:
                net.meet()
            while steps and steps[0][0] <= op[2] + 0.01:
                _, s, ph = steps.pop(0)
                red.step(s, ph)
    left = {}
    for _, s, ph in steps:
        left.setdefault(s, []).append(ph)
    while any(left.values()):
        for s in sorted(left, reverse=ORDER):
            if left[s]:
                red.step(s, left[s].pop(0))
    if comm:
        for c in red.sent:
            c.wait_send()


def gram_reduce(u, comm=True):
    v = pl.BlockSpec(memory_space=pltpu.VMEM)
    n = len(STAGES)
    V = pltpu.VMEM
    kw = dict(collective_id=0, has_side_effects=True) if comm else {}
    return pl.pallas_call(
        functools.partial(gram_reduce_kernel, comm=comm),
        out_shape=jax.ShapeDtypeStruct((10, 512, 128), F32),
        in_specs=[pl.BlockSpec(memory_space=pl.ANY)], out_specs=v,
        scratch_shapes=[
            V((1024, 2 * KH), F32), V((4, 512, 2 * KH), BF), V((10, 512, 128), F32),
            V((10, 256, 128), F32), V((10, 256, 128), F32),
            V((2, 3, 10, 32, 128), F32), V((2, 10, 32, 128), F32),
            V((2, 3, 10, 8, 128), F32), V((2, 10, 8, 128), F32), V((2, 3, 10, 8, 128), F32),
            pltpu.SemaphoreType.DMA((5,)), pltpu.SemaphoreType.DMA((n, 32)), pltpu.SemaphoreType.DMA((n, 32)),
        ],
        compiler_params=pltpu.CompilerParams(vmem_limit_bytes=46 << 20, **kw),
    )(u)


def per_device(unfolding, start_basis):
    packed = gram_reduce(unfolding)
    return iterate_project(packed, start_basis, unfolding)


def solution(mesh):
    in_specs = (P(None, ("grp", "in")), P())
    out_specs = (P(), P(None, ("grp", "in")))
    return jax.shard_map(
        per_device, mesh=mesh, in_specs=in_specs, out_specs=out_specs, check_vma=False
    )
```

```python
import functools

import jax
import jax.numpy as jnp
from jax import lax
from jax.experimental import pallas as pl
from jax.experimental.pallas import tpu as pltpu
from jax.sharding import PartitionSpec as P

HI = lax.Precision.HIGHEST
F32 = jnp.float32
BF = jnp.bfloat16

def split(x):
    hi = x.astype(BF)
    return hi, (x - hi.astype(F32)).astype(BF)

def dg(a, b, ca, cb):
    return lax.dot_general(a, b, (((ca,), (cb,)), ((), ())), preferred_element_type=F32)

GROUP = 8


def eliminate(a_ref, q_ref, w_ref):
    sub = lax.broadcasted_iota(jnp.int32, (8, 128), 0)
    lane = lax.broadcasted_iota(jnp.int32, (8, 128), 1)
    wide = lambda v: jnp.broadcast_to(v, (8, 128))
    row = lambda v, r: wide(v[r:r + 1, :])
    col = lambda v, c: wide(v[:, c:c + 1])
    M = [a_ref[8 * p:8 * p + 8, :] for p in range(16)]
    on = [lane == sub + 8 * p for p in range(16)]
    diag = jnp.where(on[0], M[0], 0.0)
    for p in range(1, 16):
        diag = diag + jnp.where(on[p], M[p], 0.0)
    scale = wide(1.0 / jnp.sqrt(jnp.sum(diag, axis=0, keepdims=True)))
    Q = [jnp.where(on[p], scale, 0.0) for p in range(16)]
    for p in range(16):
        M[p] = M[p] * scale * wide(jnp.sum(Q[p], axis=1, keepdims=True))
    done = []
    for p in range(16):
        P, R = M[p], Q[p]
        last = p == 15
        edge = p % GROUP == GROUP - 1
        N, S = (None, None) if edge else (M[p + 1], Q[p + 1])
        cs = [col(P, 8 * p + c) for c in range(8)] if p % GROUP == 0 else gs
        es, gs = [], []
        if not edge:
            es = [col(N, 8 * p + c) for c in range(8)]
            gs = [col(N, 8 * p + 8 + c) for c in range(8)]
        dv = rv = tv = jnp.zeros((8, 128), F32)
        for r in range(0, 8, 2):
            a, b, d = row(cs[r], r), row(cs[r], r + 1), row(cs[r + 1], r + 1)
            det = a * d - b * b
            rdet = 1.0 / det
            ra = 1.0 / a
            dv = jnp.where(sub == r, a, jnp.where(sub == r + 1, det * ra, dv))
            rv = jnp.where(sub == r, ra, jnp.where(sub == r + 1, a * rdet, rv))
            tv = jnp.where(sub == r + 1, b * ra, tv)
            sets = []
            if r < 6:
                below = sub > r + 1
                sets.append((jnp.where(below, d * cs[r] - b * cs[r + 1], 0.0),
                             jnp.where(below, a * cs[r + 1] - b * cs[r], 0.0)))
            if not edge:
                sets.append((d * es[r] - b * es[r + 1], a * es[r + 1] - b * es[r]))
            p0, p1, q0, q1 = row(P, r), row(P, r + 1), row(R, r), row(R, r + 1)
            for k in range(r + 2, 8):
                s0, s1 = row(cs[k], r), row(cs[k], r + 1)
                if not edge:
                    n0, n1 = sets[-1]
                    es[k] = es[k] - rdet * (n0 * s0 + n1 * s1)
                n0, n1 = sets[0]
                cs[k] = cs[k] - rdet * (n0 * s0 + n1 * s1)
            for k in range(8 if not edge else 0):
                s0, s1 = row(es[r], k), row(es[r + 1], k)
                n0, n1 = sets[-1]
                gs[k] = gs[k] - rdet * (n0 * s0 + n1 * s1)
            if r < 6:
                n0, n1 = sets[0]
                P = P - rdet * (n0 * p0 + n1 * p1)
                R = R - rdet * (n0 * q0 + n1 * q1)
            if not edge:
                n0, n1 = sets[-1]
                N = N - rdet * (n0 * p0 + n1 * p1)
                S = S - rdet * (n0 * q0 + n1 * q1)
        P = P - tv * pltpu.roll(P, 1, 0)
        R = R - tv * pltpu.roll(R, 1, 0)
        w_ref[8 * p:8 * p + 8, :] = R * (1.0 / jnp.sqrt(dv))
        if not edge:
            M[p + 1], Q[p + 1] = N, S
        done.append((P, R, P * rv))
        group = p // GROUP
        stop = GROUP * group + GROUP
        if p + 2 < min(stop, 16):
            T = jnp.transpose(P * rv)
            pr = [row(P, r) for r in range(8)]
            qr = [row(R, r) for r in range(8)]
            for i in range(p + 2, stop):
                for r in range(8):
                    mm = wide(T[8 * i:8 * i + 8, r:r + 1])
                    M[i] = M[i] - mm * pr[r]
                    Q[i] = Q[i] - mm * qr[r]
        if p == stop - 1 and not last:
            parts = done[GROUP * group:]
            left = jnp.concatenate([v[2] for v in parts], axis=0)
            right = jnp.concatenate([jnp.concatenate(v[:2], axis=1) for v in parts], axis=0)
            upd = lax.dot_general(left, right, (((0,), (0,)), ((), ())), precision=HI, preferred_element_type=F32)
            for i in range(stop, 16):
                M[i] = M[i] - upd[8 * i:8 * i + 8, :128]
                Q[i] = Q[i] - upd[8 * i:8 * i + 8, 128:]


ITERS = 3


def tail_kernel(x_ref, s_ref, u_hbm, f_ref, o_hbm, ghi, glo, img, a_ref, q_ref, w_ref, u_ref, f2, out, lsem, osem):
    pieces = [slice(c, c + 512) for c in range(0, 4096, 512)]
    loads = [pltpu.make_async_copy(u_hbm.at[:, c], u_ref.at[:, c], lsem.at[n]) for n, c in enumerate(pieces)]
    for c in loads:
        c.start()
    k = 0
    for j in range(4):
        for i in range(j + 1):
            blk = jnp.concatenate([x_ref[k, :256, :], x_ref[k, 256:, :]], axis=1)
            if i == j:
                blk = 0.5 * (blk + blk.T)
            hi, lo = split(blk)
            ghi[256*i:256*i+256, 256*j:256*j+256] = hi
            glo[256*i:256*i+256, 256*j:256*j+256] = lo
            if i != j:
                ghi[256*j:256*j+256, 256*i:256*i+256] = hi.T
                glo[256*j:256*j+256, 256*i:256*i+256] = lo.T
            k += 1
    f_ref[...] = s_ref[...]

    def body(t, _):
        bh, bl = split(f_ref[...])
        b2 = jnp.concatenate([bh, bl], axis=1)
        for i in range(4):
            r2 = dg(ghi[256*i:256*i+256, :], b2, 1, 0)
            r1 = dg(glo[256*i:256*i+256, :], bh, 1, 0)
            img[256*i:256*i+256, :] = r2[:, :128] + (r2[:, 128:] + r1)
        im = img[...]
        a_ref[...] = lax.dot_general(im, im, (((0,), (0,)), ((), ())), precision=HI, preferred_element_type=F32)
        eliminate(a_ref, q_ref, w_ref)
        ih, il = split(img[...])
        wh, wl = split(w_ref[...])
        r2 = dg(ih, jnp.concatenate([wh, wl], axis=0), 1, 1)
        f_ref[...] = r2[:, :128] + (r2[:, 128:] + dg(il, wh, 1, 1))
        return 0

    lax.fori_loop(0, ITERS, body, 0)
    fh, fl = split(f_ref[...].T)
    f2[:128, :] = fh
    f2[128:, :] = fl
    for c in loads:
        c.wait()
    stores = []
    for n, c in enumerate(pieces):
        h, l = split(u_ref[:, c])
        r = dg(f2[...], h, 1, 0)
        out[:, c] = r[:128, :] + (r[128:, :] + dg(f2[:128, :], l, 1, 0))
        if n % 2 == 1:
            two = slice(c.stop - 1024, c.stop)
            stores.append(pltpu.make_async_copy(out.at[:, two], o_hbm.at[:, two], osem.at[n // 2]))
            stores[-1].start()
    for c in stores:
        c.wait()


def iterate_project(x, s, u):
    v, anyw = pl.BlockSpec(memory_space=pltpu.VMEM), pl.BlockSpec(memory_space=pl.ANY)
    V = pltpu.VMEM
    return pl.pallas_call(
        tail_kernel,
        out_shape=(jax.ShapeDtypeStruct((1024, 128), F32), jax.ShapeDtypeStruct((128, 4096), F32)),
        in_specs=[v, v, anyw], out_specs=(v, anyw),
        scratch_shapes=[V((1024, 1024), BF), V((1024, 1024), BF), V((1024, 128), F32),
                        V((128, 128), F32), V((128, 128), F32), V((128, 128), F32),
                        V((1024, 4096), F32), V((256, 1024), BF), V((128, 4096), F32),
                        pltpu.SemaphoreType.DMA((8,)), pltpu.SemaphoreType.DMA((4,))],
        compiler_params=pltpu.CompilerParams(vmem_limit_bytes=50 << 20),
    )(x, s, u)

MESH = pl.DeviceIdType.MESH
BLOCKS = [(i, j) for j in range(4) for i in range(j + 1)]
STAGES = ((0, 3), (3, 6), (6, 8), (8, 10))
KH = 2048

LAT = (2.0, 3.9, 3.0)


class Net:
    def __init__(self):
        self.y = lax.axis_index("grp")
        self.inn = lax.axis_index("in")
        self.core = lax.rem(self.inn, 2)
        self.x = lax.rem(self.inn // 2, 4)
        self.z = self.inn // 8

    def axis(self, number):
        a = lax.rem(number, 3)
        ex, ey, ez = (2 - a) * (1 - a) // 2, a * (2 - a), a * (a - 1) // 2
        return Axis(self, ex, ey, ez)

    def twin(self):
        return (self.y, self.inn + 1 - 2 * self.core)

    def greet(self):
        b = pltpu.get_barrier_semaphore()
        pl.semaphore_signal(b, inc=1, device_id=self.twin(), device_id_type=MESH)
        for e in ((1, 0, 0), (0, 1, 0), (0, 0, 1)):
            for d in (1, 2, 3):
                pl.semaphore_signal(b, inc=1, device_id=Axis(self, *e).peer(d), device_id_type=MESH)

    def meet(self):
        pl.semaphore_wait(pltpu.get_barrier_semaphore(), 10)


class Axis:
    def __init__(self, net, ex, ey, ez):
        self.net, self.e = net, (ex, ey, ez)
        self.me = net.x * ex + net.y * ey + net.z * ez

    def at(self, d):
        return lax.rem(self.me + d, 4)

    def peer(self, d):
        ex, ey, ez = self.e
        delta = self.at(d) - self.me
        return (self.net.y + delta * ey, self.net.inn + delta * (2 * ex + 8 * ez))


def rows(start, n):
    return pl.ds(pl.multiple_of(start, n), n)


class Reduce:
    def __init__(self, net, x, o, b0, a0, b1, a1, b2, a2, b3, ssem, rsem):
        self.net, self.x, self.o = net, x, o
        self.b0, self.a0, self.b1, self.a1, self.b2, self.a2, self.b3 = b0, a0, b1, a1, b2, a2, b3
        self.ssem, self.rsem = ssem, rsem
        self.flying, self.sent = {}, []
        self.axes = {}
        base = [net.axis(2 * net.core + e) for e in range(3)]
        for s in range(len(STAGES)):
            for p in range(2):
                self.axes[s, p] = [base[(s + p + lvl) % 3] for lvl in range(3)]

    def send(self, src, dst, s, k, dev):
        c = pltpu.make_async_remote_copy(
            src_ref=src, dst_ref=dst, send_sem=self.ssem.at[s, k], recv_sem=self.rsem.at[s, k],
            device_id=dev, device_id_type=MESH,
        )
        c.start()
        self.flying.setdefault(s, []).append(c)

    def land(self, s):
        for c in self.flying.get(s, []):
            c.wait_recv()
        self.sent += self.flying.get(s, [])
        self.flying[s] = []

    def step(self, s, phase):
        u = slice(*STAGES[s])
        core = self.net.core
        self.land(s)
        if phase == 0:
            self.send(self.x.at[u, rows(256 - 256 * core, 256), :], self.b0.at[u], s, 0, self.net.twin())
            return
        if phase == 7:
            half = self.o.at[u, rows(256 * core, 256), :]
            self.send(half, half, s, 31, self.net.twin())
            return
        if phase == 8:
            return
        if phase == 1:
            self.a0[u] = self.x[u, rows(256 * core, 256), :] + self.b0[u]
        for p in range(2):
            x1, x2, x3 = self.axes[s, p]
            if phase == 1:
                for d in (1, 2, 3):
                    src = self.a0.at[u, rows(128 * p + 32 * x1.at(d), 32), :]
                    self.send(src, self.b1.at[p, d - 1, u], s, 1 + 15 * p + d - 1, x1.peer(d))
            if phase == 2:
                own = self.a0[u, rows(128 * p + 32 * x1.me, 32), :]
                self.a1[p, u] = own + (self.b1[p, 0, u] + (self.b1[p, 1, u] + self.b1[p, 2, u]))
                for d in (1, 2, 3):
                    src = self.a1.at[p, u, rows(8 * x2.at(d), 8), :]
                    self.send(src, self.b2.at[p, d - 1, u], s, 4 + 15 * p + d - 1, x2.peer(d))
            if phase == 3:
                own = self.a1[p, u, rows(8 * x2.me, 8), :]
                self.a2[p, u] = own + (self.b2[p, 0, u] + (self.b2[p, 1, u] + self.b2[p, 2, u]))
                for d in (1, 2, 3):
                    self.send(self.a2.at[p, u], self.b3.at[p, d - 1, u], s, 7 + 15 * p + d - 1, x3.peer(d))
            if phase == 4:
                here = self.o.at[u, rows(256 * core + 128 * p + 32 * x1.me + 8 * x2.me, 8), :]
                here[...] = self.ordered(p, u, x3)
                for d in (1, 2, 3):
                    self.send(here, here, s, 10 + 15 * p + d - 1, x2.peer(d))
            if phase == 5:
                here = self.o.at[u, rows(256 * core + 128 * p + 32 * x1.me, 32), :]
                for d in (1, 2, 3):
                    self.send(here, here, s, 13 + 15 * p + d - 1, x1.peer(d))

    def ordered(self, p, u, axis):
        own, t1, t2, t3 = self.a2[p, u], self.b3[p, 0, u], self.b3[p, 1, u], self.b3[p, 2, u]
        even = lax.rem(axis.me, 2) == 0
        near = jnp.where(even, t3, t1)
        far = jnp.where(even, t1, t3)
        return (own + near) + (t2 + far)


PROGRAM = (
    ("wait", 0), ("convert", 0, 0),
    ("wait", 1), ("convert", 0, 1), ("dot", 0, 0), ("dot", 0, 1),
    ("wait", 2), ("convert", 1, 0), ("dot", 1, 0), ("dot", 2, 0), ("convert", 1, 1),
    ("wait", 3), ("dot", 1, 1), ("dot", 2, 1), ("convert", 2, 0), ("check", 3, 7.5),
    ("wait", 4), ("convert", 2, 1), ("dot", 3, 2), ("dot", 4, 2), ("convert", 3, 0), ("check", 5, 11.0),
    ("dot", 5, 2), ("convert", 3, 1), ("check", 6, 12.4),
    ("dot", 6, 2), ("dot", 7, 2), ("check", 8, 15.7),
    ("dot", 8, 2), ("check", 9, 17.4),
    ("dot", 9, 2), ("check", 10, 18.5),
)


def plan():
    ready = {}
    for op in PROGRAM:
        if op[0] == "check":
            for k in range(op[1]):
                ready.setdefault(k, op[2])
    steps = []
    for s, (a, b) in enumerate(STAGES):
        m = b - a
        t = ready[b - 1]
        cost = (LAT[0] + 0.3 * m, LAT[1] + 0.6 * m, LAT[1] + 0.2 * m, LAT[2] + 0.2 * m, LAT[1] + 0.2 * m, LAT[1] + 0.6 * m, 0.0, LAT[0] + 0.3 * m, 0.0)
        for ph in (0, 1, 2, 3, 4, 5, 7, 8):
            steps.append((t, s, ph))
            t += cost[ph]
    return sorted(steps)


def gram_reduce_kernel(u_hbm, o_ref, stg, hl, x, b0, a0, b1, a1, b2, a2, b3, lsem, ssem, rsem, *, comm=True):
    cuts = [(0, 256, 0, 2048), (0, 256, 2048, 4096), (256, 512, 0, 4096), (512, 768, 0, 4096), (768, 1024, 0, 4096)]
    loads = []
    for n, (ra, rb, ca, cb) in enumerate(cuts):
        loads.append(pltpu.make_async_copy(u_hbm.at[ra:rb, ca:cb], stg.at[ra:rb, ca:cb], lsem.at[n]))
        loads[-1].start()
    steps = []
    if comm:
        net = Net()
        net.greet()
        red = Reduce(net, x, o_ref, b0, a0, b1, a1, b2, a2, b3, ssem, rsem)
        steps = plan()

    def convert(i, h):
        for c in range(KH * h, KH * h + KH, 256):
            hi, lo = split(stg[256 * i:256 * i + 256, c:c + 256])
            hl[i, :256, c:c + 256] = hi
            hl[i, 256:, c:c + 256] = lo

    dst = x if comm else o_ref

    def dot(k, h):
        i, j = BLOCKS[k]
        ks = slice(0, 2 * KH) if h == 2 else slice(KH * h, KH * h + KH)
        if i == j:
            r = dg(hl[i, :256, ks], hl[j, :256, ks], 1, 1) + 2.0 * dg(hl[i, :256, ks], hl[j, 256:, ks], 1, 1)
        else:
            r2 = dg(hl[i, :, ks], hl[j, :256, ks], 1, 1)
            r = r2[:256] + (r2[256:] + dg(hl[i, :256, ks], hl[j, 256:, ks], 1, 1))
        if h == 1:
            dst[k, :256, :] += r[:, :128]
            dst[k, 256:, :] += r[:, 128:]
        else:
            dst[k, :256, :] = r[:, :128]
            dst[k, 256:, :] = r[:, 128:]

    for op in PROGRAM:
        if op[0] == "wait":
            loads[op[1]].wait()
        elif op[0] == "convert":
            convert(*op[1:])
        elif op[0] == "dot":
            dot(*op[1:])
        else:
            if comm and op[1] == 3:
                net.meet()
            while steps and steps[0][0] <= op[2] + 0.01:
                _, s, ph = steps.pop(0)
                red.step(s, ph)
    left = {}
    for _, s, ph in steps:
        left.setdefault(s, []).append(ph)
    while any(left.values()):
        for s in sorted(left, reverse=False):
            if left[s]:
                red.step(s, left[s].pop(0))
    if comm:
        for c in red.sent:
            c.wait_send()


def gram_reduce(u, comm=True):
    v = pl.BlockSpec(memory_space=pltpu.VMEM)
    n = len(STAGES)
    V = pltpu.VMEM
    kw = dict(collective_id=0, has_side_effects=True) if comm else {}
    return pl.pallas_call(
        functools.partial(gram_reduce_kernel, comm=comm),
        out_shape=jax.ShapeDtypeStruct((10, 512, 128), F32),
        in_specs=[pl.BlockSpec(memory_space=pl.ANY)], out_specs=v,
        scratch_shapes=[
            V((1024, 2 * KH), F32), V((4, 512, 2 * KH), BF), V((10, 512, 128), F32),
            V((10, 256, 128), F32), V((10, 256, 128), F32),
            V((2, 3, 10, 32, 128), F32), V((2, 10, 32, 128), F32),
            V((2, 3, 10, 8, 128), F32), V((2, 10, 8, 128), F32), V((2, 3, 10, 8, 128), F32),
            pltpu.SemaphoreType.DMA((5,)), pltpu.SemaphoreType.DMA((n, 32)), pltpu.SemaphoreType.DMA((n, 32)),
        ],
        compiler_params=pltpu.CompilerParams(vmem_limit_bytes=46 << 20, **kw),
    )(u)


def per_device(unfolding, start_basis):
    packed = gram_reduce(unfolding)
    return iterate_project(packed, start_basis, unfolding)


def solution(mesh):
    in_specs = (P(None, ("grp", "in")), P())
    out_specs = (P(), P(None, ("grp", "in")))
    return jax.shard_map(
        per_device, mesh=mesh, in_specs=in_specs, out_specs=out_specs, check_vma=False
    )
```
